256 devices in a mesh: lon: 32 (over y, z), lat: 8 (over x, core).
Axes of the slice: x: 4, y: 4, z: 8, core: 2. Of those that a mesh axis runs over, the one named last changes fastest.
Arguments:
- surface_adjoint: float32 [2048, 32768], P('lat', 'lon'), may hold values from -6 to 6
- east_adjoint: float32 [2048, 32768], P('lat', 'lon'), may hold values from -6 to 6
- north_adjoint: float32 [2048, 32768], P('lat', 'lon'), may hold values from -6 to 6
- water_depth: float32 [2048, 32768], P('lat', 'lon'), may hold values from 0.3 to 1
- wet_mask: int32 [2048, 32768], P('lat', 'lon'), may hold values 0 or 1
- control_active: int32 [128, 2048], P('lat', 'lon'), may hold values 0 or 1
Outputs:
- surface_after: float32 [2048, 32768], P('lat', 'lon')
- east_after: float32 [2048, 32768], P('lat', 'lon')
- north_after: float32 [2048, 32768], P('lat', 'lon')
- uplift_grad: float32 [128, 2048], P('lat', 'lon')
The draws below stay inside these ranges and needn't reach their ends.
All inputs are finite; a program needn't handle non-finite values. No bound on the sum of `wet_mask` or of `control_active` on one device may be relied on, other than what follows from the above.
Results may differ from the reference program's by a relative error of at most 0.00021.
Values sent between devices are 32-bit elements; how exact they have to be, the bound alone decides.
A program may use at most 64 MiB of HBM per device.

```python
import math
import jax
import jax.numpy as jnp
from jax import lax

SPACING = 16
STEPS = 3
NLAT = 2048
NLON = 32768
KALL = 128
KOLL = 2048


def set_ends(drawn, stream_key, least, high):
    extent = drawn.shape
    spot = [jax.random.randint(jax.random.fold_in(stream_key, axis), (), 0, extent[axis]) for axis in range(len(extent))]
    drawn = drawn.at[tuple(spot)].set(least)
    longest = extent.index(max(extent))
    spot[longest] = (spot[longest] + 1) % extent[longest]
    return drawn.at[tuple(spot)].set(high)


def levels(key, dims, cuts, smallest, high):
    loudness = 1.0
    for dim, shards_of in cuts:
        heights = jax.random.uniform(jax.random.fold_in(jax.random.fold_in(key, 6), dim), (shards_of,), jnp.float32, smallest / len(cuts), high / len(cuts))
        loudness = loudness * jnp.repeat(jnp.exp(heights), dims[dim] // shards_of).reshape((-1,) + (1,) * (len(dims) - 1 - dim))
    return loudness


def noise(own_key, shape, deviation, bound, cuts=(), kind=jnp.bfloat16):
    gain = levels(own_key, shape, cuts, -0.22, 0.18) if cuts else 1.0
    result = jax.random.normal(own_key, shape, jnp.float32) * deviation * gain
    return jnp.minimum(jnp.maximum(result, -bound), bound).astype(kind)


def setup_inputs(seed: int = 0) -> dict:
    keys = jax.random.split(jax.random.key(seed), 7)
    surface_adjoint = noise(keys[0], (NLAT, NLON), 1.0, 6.0, ((0, 8), (1, 32)), jnp.float32)
    east_adjoint = noise(keys[1], (NLAT, NLON), 1.0, 6.0, ((0, 8), (1, 32)), jnp.float32)
    north_adjoint = noise(keys[2], (NLAT, NLON), 1.0, 6.0, ((0, 8), (1, 32)), jnp.float32)
    water_depth = jnp.clip(jnp.exp(math.log(1.0) - 1.2039728 * jax.random.uniform(keys[3], (NLAT, NLON), jnp.float32) ** levels(keys[3], (NLAT, NLON), ((0, 8), (1, 32)), -0.2, 0.2)), 0.3, 1.0)
    wet_mask = set_ends((jax.random.randint(keys[4], (NLAT, NLON), 0, 10) < 9).astype(jnp.int32), jax.random.fold_in(keys[4], 1), 0, 1)
    control_active = set_ends((jax.random.randint(keys[5], (KALL, KOLL), 0, 4) < 3).astype(jnp.int32), jax.random.fold_in(keys[5], 1), 0, 1)
    return dict(surface_adjoint=surface_adjoint, east_adjoint=east_adjoint, north_adjoint=north_adjoint, water_depth=water_depth, wet_mask=wet_mask, control_active=control_active)


courant = 0.5


def from_east(field):
    return jnp.pad(field[:, 1:], ((0, 0), (0, 1)))


def west_incoming(field):
    return jnp.pad(field[:, :-1], ((0, 0), (1, 0)))


def from_north(field):
    return jnp.pad(field[1:, :], ((0, 1), (0, 0)))


def from_south(field):
    return jnp.pad(field[:-1, :], ((1, 0), (0, 0)))


def march_steps(surface_height, eastward, northward, wet_depth, wet_fraction):
    for step in range(STEPS):
        eastward = wet_fraction * (eastward + courant * wet_depth * (from_east(surface_height) - west_incoming(surface_height)))
        northward = wet_fraction * (northward + courant * wet_depth * (from_north(surface_height) - from_south(surface_height)))
        surface_height = wet_fraction * (surface_height + courant * ((from_east(eastward) - west_incoming(eastward)) + (from_north(northward) - from_south(northward))))
    return surface_height, eastward, northward


def spline_weight(arg):
    mag = jnp.abs(arg)
    inner = 2.0 / 3.0 - mag * mag + 0.5 * mag * mag * mag
    outer = (2.0 - mag) * (2.0 - mag) * (2.0 - mag) / 6.0
    return jnp.where(mag < 1.0, inner, jnp.where(mag < 2.0, outer, 0.0 * mag))


def move_rows(block, offset):
    if offset > 0:
        return jnp.pad(block, ((offset, 0), (0, 0)))[:-offset]
    if offset < 0:
        return jnp.pad(block, ((0, -offset), (0, 0)))[-offset:]
    return block


def reference(surface_adjoint, east_adjoint, north_adjoint, water_depth, wet_mask, control_active):
    wet_fraction = wet_mask.astype(jnp.float32)
    wet_depth = water_depth * wet_fraction
    surface_height, eastward, northward = march_steps(surface_adjoint, east_adjoint, north_adjoint, wet_depth, wet_fraction)
    lag = (jnp.arange(5, dtype=jnp.float32) - 2.0)[:, None]
    inside = (jnp.arange(SPACING, dtype=jnp.float32)[None, :] + 0.5) / SPACING
    weight_table = spline_weight(inside - 0.5 - lag)

    def band(block):
        cubic_basis = block.reshape(SPACING, KOLL, SPACING)
        half_width = jnp.einsum('lq,qgw->lgw', weight_table, cubic_basis, precision=lax.Precision.HIGHEST)
        return jnp.einsum('dbr,er->dbe', half_width, weight_table, precision=lax.Precision.HIGHEST)

    parts = lax.map(band, surface_height.reshape(KALL, SPACING, NLON))
    sums = jnp.zeros((KALL, KOLL), jnp.float32)
    for lag_row in range(5):
        for lag_col in range(5):
            piece = move_rows(parts[:, lag_row, :, lag_col], lag_row - 2)
            piece = move_rows(piece.T, lag_col - 2).T
            sums = sums + piece
    uplift_grad = sums * control_active.astype(jnp.float32) / SPACING
    return surface_height, eastward, northward, uplift_grad
```

```python
import jax
import jax.numpy as jnp
from jax import lax
from jax.experimental import pallas as pl
from jax.experimental.pallas import tpu as pltpu
from jax.sharding import PartitionSpec as P

SPACING = 16
LANES = 128
HALO = 8
BLOCK = 16
F32 = jnp.float32

SOUTH, NORTH, WEST, EAST = (-1, 0), (1, 0), (0, -1), (0, 1)
SW, SE, NW, NE = (-1, -1), (-1, 1), (1, -1), (1, 1)
NEIGHBOURS = (SOUTH, NORTH, WEST, EAST, SW, SE, NW, NE)


def spline_weight(arg):
    mag = jnp.abs(arg)
    inner = 2.0 / 3.0 - mag * mag + 0.5 * mag * mag * mag
    outer = (2.0 - mag) * (2.0 - mag) * (2.0 - mag) / 6.0
    return jnp.where(mag < 1.0, inner, jnp.where(mag < 2.0, outer, 0.0 * mag))


def lanes_of(shape):
    return lax.broadcasted_iota(jnp.int32, shape, 1)


def left(x, k):
    return pltpu.roll(x, x.shape[1] - k, axis=1)


def right(x, k):
    return pltpu.roll(x, k, axis=1)


def below(x, following, k):
    return jnp.concatenate([x, following], axis=0)[k : k + x.shape[0]]


def above(preceding, x, k):
    return jnp.concatenate([preceding, x], axis=0)[HALO - k : HALO - k + x.shape[0]]


def kernel(
    s_in, e_in, n_in, d_in, w_in, active,
    s_out, e_out, n_out, grad,
    S, E, N, CX, CY, M, W, R, PART,
    pack_w, pack_e, got_w, got_e, corner, fold,
    load_sem, send_sem, recv_sem,
):
    rows, cols = s_out.shape
    tall = rows + 2 * HALO
    tiles = cols // LANES
    quarter = rows // 4
    nlat, nlon = lax.axis_size("lat"), lax.axis_size("lon")
    lat, lon = lax.axis_index("lat"), lax.axis_index("lon")

    def has(offset):
        a, b = lat + offset[0], lon + offset[1]
        return (a >= 0) & (a < nlat) & (b >= 0) & (b < nlon)

    def opposite(offset):
        return (-offset[0], -offset[1])

    regions = (
        (0, rows, 0, LANES),
        (0, rows, cols - LANES, LANES),
        (0, HALO, LANES, cols - 2 * LANES),
        (rows - HALO, HALO, LANES, cols - 2 * LANES),
        (HALO, rows - 2 * HALO, LANES, cols - 2 * LANES),
    )
    loads = []
    for k, (r, h, c, w) in enumerate(regions):
        group = []
        for a, (src, dst) in enumerate(((w_in, W), (d_in, CX), (e_in, E), (n_in, N), (s_in, S))):
            base = 0 if dst is W else HALO
            group.append(
                pltpu.make_async_copy(
                    src.at[pl.ds(r, h), pl.ds(c, w)],
                    dst.at[pl.ds(base + r, h), pl.ds(c, w)],
                    load_sem.at[k * 5 + a],
                )
            )
        loads.append(group)
    for group in loads:
        for copy in group:
            copy.start()

    barrier = pltpu.get_barrier_semaphore()
    count = jnp.int32(0)
    for offset in NEIGHBOURS:
        count = count + has(offset).astype(jnp.int32)

        @pl.when(has(offset))
        def _(offset=offset):
            pl.semaphore_signal(
                barrier, inc=1,
                device_id={"lat": lat + offset[0], "lon": lon + offset[1]},
                device_id_type=pl.DeviceIdType.MESH,
            )

    def messages(items, first):
        made = []
        for k, (src, dst, offset) in enumerate(items):
            made.append((
                pltpu.make_async_remote_copy(
                    src_ref=src, dst_ref=dst,
                    send_sem=send_sem.at[first + k], recv_sem=recv_sem.at[first + k],
                    device_id={"lat": lat + offset[0], "lon": lon + offset[1]},
                    device_id_type=pl.DeviceIdType.MESH,
                ),
                offset,
            ))
        return made

    def start(made):
        for copy, offset in made:
            @pl.when(has(offset))
            def _(copy=copy):
                copy.start()

    def finish(made):
        for copy, offset in made:
            @pl.when(has(opposite(offset)))
            def _(copy=copy):
                copy.wait_recv()

            @pl.when(has(offset))
            def _(copy=copy):
                copy.wait_send()

    fields = (S, E, N, CX)
    body = pl.ds(0, cols)
    low, high = pl.ds(0, HALO), pl.ds(HALO + rows, HALO)
    first_rows, last_rows = pl.ds(HALO, HALO), pl.ds(rows, HALO)
    side = [(pack_w, got_e, WEST), (pack_e, got_w, EAST)]
    side += [
        (pack_w.at[pl.ds(0, HALO)], corner.at[3], SW),
        (pack_e.at[pl.ds(0, HALO)], corner.at[2], SE),
        (pack_w.at[pl.ds(quarter - HALO, HALO)], corner.at[1], NW),
        (pack_e.at[pl.ds(quarter - HALO, HALO)], corner.at[0], NE),
    ]
    rim = [(f.at[first_rows, body], f.at[high, body], SOUTH) for f in fields]
    rim += [(f.at[last_rows, body], f.at[low, body], NORTH) for f in fields]
    rim = messages(rim, 0)
    side = messages(side, len(rim))

    @pl.when(lat == 0)
    def _():
        for f in fields:
            f[0:HALO, 0:cols] = jnp.zeros((HALO, cols), F32)
        fold[0] = jnp.zeros_like(fold[0])

    @pl.when(lat == nlat - 1)
    def _():
        for f in fields:
            f[HALO + rows : tall, 0:cols] = jnp.zeros((HALO, cols), F32)
        fold[1] = jnp.zeros_like(fold[1])

    for pack, offset, k in ((got_w, WEST, 2), (got_e, EAST, 3)):
        @pl.when(jnp.logical_not(has(offset)))
        def _(pack=pack, k=k):
            pack[...] = jnp.zeros_like(pack)
            fold[k] = jnp.zeros_like(fold[k])

    for k, offset in enumerate((SW, SE, NW, NE)):
        @pl.when(jnp.logical_not(has(offset)))
        def _(k=k):
            corner[k] = jnp.zeros_like(corner[k])
            fold[4 + k] = jnp.zeros_like(fold[4 + k])

    for f in (S, N, CX):
        f[tall : tall + HALO, :] = jnp.zeros((HALO, cols + LANES), F32)
    R[...] = jnp.zeros_like(R)

    def prepare(r, h, c, w):
        here = (pl.ds(HALO + r, h), pl.ds(c, w))
        wet = W[pl.ds(r, h), pl.ds(c, w)].astype(F32)
        half = 0.5 * wet
        M[here] = half
        CX[here] = CX[here] * half
        E[here] = E[here] * wet
        N[here] = N[here] * wet

    for k in (0, 1, 2, 3):
        for copy in loads[k]:
            copy.wait()
        prepare(*regions[k])

    lane = lanes_of((quarter, LANES))
    for pack, tile, turn in ((pack_w, 0, 0), (pack_e, tiles - 1, 1)):
        total = jnp.zeros((quarter, LANES), F32)
        for a, f in enumerate(fields):
            for b in range(4):
                g = 4 * b + a
                piece = f[HALO + b * quarter : HALO + (b + 1) * quarter, tile * LANES : (tile + 1) * LANES]
                shift = 8 * (g + turn) % LANES
                piece = piece if shift == 0 else right(piece, shift)
                total = jnp.where((lane >= 8 * g) & (lane < 8 * g + 8), piece, total)
        pack[...] = total

    pl.semaphore_wait(barrier, count)
    start(side)
    start(rim)

    for copy in loads[4]:
        copy.wait()

    inner = regions[4]

    def prepare_block(j, carry):
        prepare(pl.multiple_of(HALO + j * BLOCK, HALO), BLOCK, inner[2], inner[3])
        return carry

    lax.fori_loop(0, inner[1] // BLOCK, prepare_block, 0)

    shape = (LANES, LANES)
    at = (lax.broadcasted_iota(jnp.int32, shape, 0).astype(F32) + 0.5) / SPACING
    column_weight = spline_weight(at - (lanes_of(shape).astype(F32) - 2.0 + 0.5))
    within = (lax.broadcasted_iota(jnp.int32, (BLOCK, LANES), 0).astype(F32) + 0.5) / SPACING
    row_weight = [jnp.tile(spline_weight(within + 1.0 - m), (1, tiles)) for m in range(4)]

    finish(side)
    finish(rim)

    ring = pl.ds(cols, LANES)

    def unpack(east, west, g):
        x = lanes_of(east.shape)
        e = east if g == 0 else right(east, LANES - 8 * g)
        w = right(west, (LANES - 8 * (g + 1)) % LANES)
        return jnp.where(x < 8, e, jnp.where(x >= LANES - 8, w, 0.0))

    for a, f in enumerate(fields):
        for b in range(4):
            f[HALO + b * quarter : HALO + (b + 1) * quarter, ring] = unpack(got_e[...], got_w[...], 4 * b + a)
        f[0:HALO, ring] = unpack(corner[1], corner[0], 12 + a)
        f[HALO + rows : tall, ring] = unpack(corner[3], corner[2], a)
    M[:, ring] = jnp.where(CX[0:tall, ring] > 0.0, 0.5, 0.0)
    for span in (low, high):
        M[span, body] = jnp.where(CX[span, body] > 0.0, 0.5, 0.0)

    blocks = tall // BLOCK
    wide = cols + LANES

    def advance(s, s_next, e, n, cx, cy, m, n_before, first):
        e = e + cx * (left(s, 2) - s)
        n = n + cy * (below(s, s_next, 2) - s)
        change = (e - right(e, 2)) + (n - above(n_before, n, 2))
        s = m * (s + s + change) if first else s + m * change
        return s, e, n

    def first_step(j, n_before):
        r = pl.multiple_of(j * BLOCK, BLOCK)
        here, nxt = pl.ds(r, BLOCK), pl.ds(r + BLOCK, HALO)
        depth = CX[here]
        cx = left(depth, 1)
        cy = below(depth, CX[nxt], 1)
        e = left(E[here], 1)
        n = below(N[here], N[nxt], 1)
        s, e, n = advance(S[here], S[nxt], e, n, cx, cy, M[here], n_before, True)
        S[here], E[here], N[here], CX[here], CY[here] = s, e, n, cx, cy
        return n[BLOCK - HALO :]

    def second_step(j, n_before):
        r = pl.multiple_of(j * BLOCK, BLOCK)
        here, nxt = pl.ds(r, BLOCK), pl.ds(r + BLOCK, HALO)
        s, e, n = advance(S[here], S[nxt], E[here], N[here], CX[here], CY[here], M[here], n_before, False)
        S[here], E[here], N[here] = s, e, n
        return n[BLOCK - HALO :]

    def last_step(j, carry, part=(0, BLOCK)):
        n_before, one, two, three = carry
        r = j * BLOCK if isinstance(j, int) else pl.multiple_of(j * BLOCK, BLOCK)
        here, nxt = pl.ds(r, BLOCK), pl.ds(r + BLOCK, HALO)
        s, e, n = advance(S[here], S[nxt], E[here], N[here], CX[here], CY[here], M[here], n_before, False)
        begin, end = part
        own = r - HALO + begin
        own = own if isinstance(j, int) else pl.multiple_of(own, HALO)
        dst = pl.ds(own, end - begin)
        s = s[begin:end, :cols]
        s_out[dst] = s
        e_out[dst] = right(e, 1)[begin:end, :cols]
        n_out[dst] = above(n_before, n, 1)[begin:end, :cols]
        sums = []
        for weight in row_weight:
            term = s * weight[begin:end]
            sums.append(term if end - begin == HALO else term[:HALO] + term[HALO:])
        R[pl.ds(j, 1), :] = jnp.sum(one + sums[0], axis=0, keepdims=True)
        return n[BLOCK - HALO :], two + sums[1], three + sums[2], sums[3]

    zero = jnp.zeros((HALO, wide), F32)
    lax.fori_loop(0, blocks, first_step, zero)
    lax.fori_loop(0, blocks, second_step, zero)
    none = jnp.zeros((HALO, cols), F32)
    carry = last_step(0, (zero, none, none, none), (HALO, BLOCK))
    carry = lax.fori_loop(1, blocks - 1, last_step, carry)
    carry = last_step(blocks - 1, carry, (0, HALO))
    for k in range(3):
        R[blocks + k : blocks + k + 1, :] = jnp.sum(carry[1 + k], axis=0, keepdims=True)

    points = R.shape[0]
    stacked = jnp.concatenate([R[:, t * LANES : (t + 1) * LANES] for t in range(tiles)], axis=0)
    spread = jnp.dot(stacked, column_weight, precision=lax.Precision.HIGHEST, preferred_element_type=F32)
    own = spread[0:points]
    for t in range(1, tiles):
        own = own + right(spread[t * points : (t + 1) * points], 8 * t)
    PART[...] = own

    top, bottom = pl.ds(0, HALO), pl.ds(points - HALO, HALO)
    cross = [
        (PART.at[bottom], fold.at[0, top], NORTH),
        (PART.at[top], fold.at[1, top], SOUTH),
        (PART, fold.at[2], EAST),
        (PART, fold.at[3], WEST),
        (PART.at[bottom], fold.at[4, top], NE),
        (PART.at[bottom], fold.at[5, top], NW),
        (PART.at[top], fold.at[6, top], SE),
        (PART.at[top], fold.at[7, top], SW),
    ]
    cross = messages(cross, len(rim) + len(side))
    start(cross)
    finish(cross)

    row = lax.broadcasted_iota(jnp.int32, (HALO, LANES), 0)
    lane = lanes_of((points, LANES))

    def with_rows(middle, south, north):
        south = jnp.where((row == 2) | (row == 3), south, 0.0)
        north = jnp.where(row < 2, north, 0.0)
        return jnp.concatenate(
            [middle[:HALO] + south, middle[HALO : points - HALO], middle[points - HALO :] + north], axis=0
        )

    mine = with_rows(own, fold[0, 0:HALO], fold[1, 0:HALO])
    west = with_rows(fold[2], fold[4, 0:HALO], fold[6, 0:HALO])
    east = with_rows(fold[3], fold[5, 0:HALO], fold[7, 0:HALO])
    half = cols // SPACING
    west = left(west, half)
    east = right(east, half)
    mine = mine + jnp.where((lane == 2) | (lane == 3), west, 0.0)
    mine = mine + jnp.where((lane == half) | (lane == half + 1), east, 0.0)
    inside = mine[2 : 2 + rows // SPACING, 2 : 2 + half]
    grad[...] = inside * active[...].astype(F32) / SPACING


def local(surface_adjoint, east_adjoint, north_adjoint, water_depth, wet_mask, control_active):
    rows, cols = surface_adjoint.shape
    points = rows // SPACING + 4
    points = (points + 7) // 8 * 8
    tall, wide = rows + 2 * HALO, cols + LANES
    field = pltpu.VMEM((tall + HALO, wide), F32)
    quarter = rows // 4
    whole = pl.BlockSpec(memory_space=pltpu.VMEM)
    in_hbm = pl.BlockSpec(memory_space=pltpu.HBM)
    shape = jax.ShapeDtypeStruct((rows, cols), F32)
    return pl.pallas_call(
        kernel,
        out_shape=(shape, shape, shape, jax.ShapeDtypeStruct(control_active.shape, F32)),
        in_specs=[in_hbm] * 5 + [whole],
        out_specs=(whole,) * 4,
        scratch_shapes=[
            field, field, field, field,
            pltpu.VMEM((tall, wide), F32),
            pltpu.VMEM((tall, wide), F32),
            pltpu.VMEM((rows, cols), jnp.int32),
            pltpu.VMEM((points, cols), F32),
            pltpu.VMEM((points, LANES), F32),
            pltpu.VMEM((quarter, LANES), F32),
            pltpu.VMEM((quarter, LANES), F32),
            pltpu.VMEM((quarter, LANES), F32),
            pltpu.VMEM((quarter, LANES), F32),
            pltpu.VMEM((4, HALO, LANES), F32),
            pltpu.VMEM((8, points, LANES), F32),
            pltpu.SemaphoreType.DMA((25,)),
            pltpu.SemaphoreType.DMA((22,)),
            pltpu.SemaphoreType.DMA((22,)),
        ],
        compiler_params=pltpu.CompilerParams(
            collective_id=0, has_side_effects=True, vmem_limit_bytes=32 * 1024 * 1024
        ),
    )(surface_adjoint, east_adjoint, north_adjoint, water_depth, wet_mask, control_active)


def solution(mesh):
    spec = P("lat", "lon")
    return jax.shard_map(
        local, mesh=mesh, in_specs=(spec,) * 6, out_specs=(spec,) * 4, check_vma=False
    )
```

```python
import jax
import jax.numpy as jnp
from jax import lax
from jax.experimental import pallas as pl
from jax.experimental.pallas import tpu as pltpu
from jax.sharding import PartitionSpec as P

SPACING = 16
LANES = 128
HALO = 8
BLOCK = 16
F32 = jnp.float32

SOUTH, NORTH, WEST, EAST = (-1, 0), (1, 0), (0, -1), (0, 1)
SW, SE, NW, NE = (-1, -1), (-1, 1), (1, -1), (1, 1)
NEIGHBOURS = (SOUTH, NORTH, WEST, EAST, SW, SE, NW, NE)


def spline_weight(arg):
    mag = jnp.abs(arg)
    inner = 2.0 / 3.0 - mag * mag + 0.5 * mag * mag * mag
    outer = (2.0 - mag) * (2.0 - mag) * (2.0 - mag) / 6.0
    return jnp.where(mag < 1.0, inner, jnp.where(mag < 2.0, outer, 0.0 * mag))


def lanes_of(shape):
    return lax.broadcasted_iota(jnp.int32, shape, 1)


def left(x, k):
    return pltpu.roll(x, x.shape[1] - k, axis=1)


def right(x, k):
    return pltpu.roll(x, k, axis=1)


def below(x, following, k):
    return jnp.concatenate([x, following], axis=0)[k : k + x.shape[0]]


def above(preceding, x, k):
    return jnp.concatenate([preceding, x], axis=0)[HALO - k : HALO - k + x.shape[0]]


def kernel(
    s_in, e_in, n_in, d_in, w_in, a_in,
    s_out, e_out, n_out, grad,
    S, E, N, CX, CY, M, W, R, PART, active,
    pack_w, pack_e, got_w, got_e, corner, fold,
    load_sem, send_sem, recv_sem,
):
    rows, cols = s_out.shape
    tall = rows + 2 * HALO
    tiles = cols // LANES
    quarter = rows // 4
    nlat, nlon = lax.axis_size("lat"), lax.axis_size("lon")
    lat, lon = lax.axis_index("lat"), lax.axis_index("lon")

    def has(offset):
        a, b = lat + offset[0], lon + offset[1]
        return (a >= 0) & (a < nlat) & (b >= 0) & (b < nlon)

    def opposite(offset):
        return (-offset[0], -offset[1])

    regions = (
        (0, rows, 0, LANES),
        (0, rows, cols - LANES, LANES),
        (0, HALO, LANES, cols - 2 * LANES),
        (rows - HALO, HALO, LANES, cols - 2 * LANES),
        (HALO, rows - 2 * HALO, LANES, cols - 2 * LANES),
    )
    loads = []
    for k, (r, h, c, w) in enumerate(regions):
        group = []
        for a, (src, dst) in enumerate(((w_in, W), (d_in, CX), (e_in, E), (n_in, N), (s_in, S))):
            base = 0 if dst is W else HALO
            group.append(
                pltpu.make_async_copy(
                    src.at[pl.ds(r, h), pl.ds(c, w)],
                    dst.at[pl.ds(base + r, h), pl.ds(c, w)],
                    load_sem.at[k * 5 + a],
                )
            )
        loads.append(group)
    for group in loads:
        for copy in group:
            copy.start()

    points_load = pltpu.make_async_copy(a_in, active, load_sem.at[25])
    points_load.start()

    barrier = pltpu.get_barrier_semaphore()
    count = jnp.int32(0)
    for offset in NEIGHBOURS:
        count = count + has(offset).astype(jnp.int32)

        @pl.when(has(offset))
        def _(offset=offset):
            pl.semaphore_signal(
                barrier, inc=1,
                device_id={"lat": lat + offset[0], "lon": lon + offset[1]},
                device_id_type=pl.DeviceIdType.MESH,
            )

    def messages(items, first):
        made = []
        for k, (src, dst, offset) in enumerate(items):
            made.append((
                pltpu.make_async_remote_copy(
                    src_ref=src, dst_ref=dst,
                    send_sem=send_sem.at[first + k], recv_sem=recv_sem.at[first + k],
                    device_id={"lat": lat + offset[0], "lon": lon + offset[1]},
                    device_id_type=pl.DeviceIdType.MESH,
                ),
                offset,
            ))
        return made

    def start(made):
        for copy, offset in made:
            @pl.when(has(offset))
            def _(copy=copy):
                copy.start()

    def finish(made):
        for copy, offset in made:
            @pl.when(has(opposite(offset)))
            def _(copy=copy):
                copy.wait_recv()

            @pl.when(has(offset))
            def _(copy=copy):
                copy.wait_send()

    fields = (S, E, N, CX)
    body = pl.ds(0, cols)
    low, high = pl.ds(0, HALO), pl.ds(HALO + rows, HALO)
    first_rows, last_rows = pl.ds(HALO, HALO), pl.ds(rows, HALO)
    side = [(pack_w, got_e, WEST), (pack_e, got_w, EAST)]
    side += [
        (pack_w.at[pl.ds(0, HALO)], corner.at[3], SW),
        (pack_e.at[pl.ds(0, HALO)], corner.at[2], SE),
        (pack_w.at[pl.ds(quarter - HALO, HALO)], corner.at[1], NW),
        (pack_e.at[pl.ds(quarter - HALO, HALO)], corner.at[0], NE),
    ]
    rim = [(f.at[first_rows, body], f.at[high, body], SOUTH) for f in fields]
    rim += [(f.at[last_rows, body], f.at[low, body], NORTH) for f in fields]
    rim = messages(rim, 0)
    side = messages(side, len(rim))

    @pl.when(lat == 0)
    def _():
        for f in fields:
            f[0:HALO, 0:cols] = jnp.zeros((HALO, cols), F32)
        fold[0] = jnp.zeros_like(fold[0])

    @pl.when(lat == nlat - 1)
    def _():
        for f in fields:
            f[HALO + rows : tall, 0:cols] = jnp.zeros((HALO, cols), F32)
        fold[1] = jnp.zeros_like(fold[1])

    for pack, offset, k in ((got_w, WEST, 2), (got_e, EAST, 3)):
        @pl.when(jnp.logical_not(has(offset)))
        def _(pack=pack, k=k):
            pack[...] = jnp.zeros_like(pack)
            fold[k] = jnp.zeros_like(fold[k])

    for k, offset in enumerate((SW, SE, NW, NE)):
        @pl.when(jnp.logical_not(has(offset)))
        def _(k=k):
            corner[k] = jnp.zeros_like(corner[k])
            fold[4 + k] = jnp.zeros_like(fold[4 + k])

    for f in (S, N, CX, M):
        f[tall : tall + HALO, :] = jnp.zeros((HALO, cols + LANES), F32)
    R[...] = jnp.zeros_like(R)

    def prepare(r, h, c, w):
        here = (pl.ds(HALO + r, h), pl.ds(c, w))
        wet = W[pl.ds(r, h), pl.ds(c, w)].astype(F32)
        half = 0.5 * wet
        M[here] = half
        CX[here] = CX[here] * half

    for k in (0, 1, 2, 3):
        for copy in loads[k]:
            copy.wait()
        prepare(*regions[k])

    lane = lanes_of((quarter, LANES))
    for pack, tile, turn in ((pack_w, 0, 0), (pack_e, tiles - 1, 1)):
        total = jnp.zeros((quarter, LANES), F32)
        for a, f in enumerate(fields):
            for b in range(4):
                g = 4 * b + a
                piece = f[HALO + b * quarter : HALO + (b + 1) * quarter, tile * LANES : (tile + 1) * LANES]
                shift = 8 * (g + turn) % LANES
                piece = piece if shift == 0 else right(piece, shift)
                total = jnp.where((lane >= 8 * g) & (lane < 8 * g + 8), piece, total)
        pack[...] = total

    pl.semaphore_wait(barrier, count)
    start(side)
    start(rim)

    for copy in loads[4]:
        copy.wait()

    inner = regions[4]

    def prepare_block(j, carry):
        prepare(pl.multiple_of(HALO + j * BLOCK, HALO), BLOCK, inner[2], inner[3])
        return carry

    lax.fori_loop(0, inner[1] // BLOCK, prepare_block, 0)

    shape = (LANES, LANES)
    at = (lax.broadcasted_iota(jnp.int32, shape, 0).astype(F32) + 0.5) / SPACING
    column_weight = spline_weight(at - (lanes_of(shape).astype(F32) - 2.0 + 0.5))
    finish(side)
    finish(rim)

    ring = pl.ds(cols, LANES)

    def unpack(east, west, g):
        x = lanes_of(east.shape)
        e = east if g == 0 else right(east, LANES - 8 * g)
        w = right(west, (LANES - 8 * (g + 1)) % LANES)
        return jnp.where(x < 8, e, jnp.where(x >= LANES - 8, w, 0.0))

    for a, f in enumerate(fields):
        for b in range(4):
            f[HALO + b * quarter : HALO + (b + 1) * quarter, ring] = unpack(got_e[...], got_w[...], 4 * b + a)
        f[0:HALO, ring] = unpack(corner[1], corner[0], 12 + a)
        f[HALO + rows : tall, ring] = unpack(corner[3], corner[2], a)
    M[0:tall, ring] = jnp.where(CX[0:tall, ring] > 0.0, 0.5, 0.0)
    for span in (low, high):
        M[span, body] = jnp.where(CX[span, body] > 0.0, 0.5, 0.0)

    count_tiles = tiles + 1

    def spread_of(x, k, height):
        return [pltpu.roll(v, k % LANES, axis=1) for v in x], lanes_of((height, LANES))

    def from_right(x, k):
        turned, at = spread_of(x, -k, x[0].shape[0])
        n = len(x)
        return [jnp.where(at < LANES - k, turned[t], turned[(t + 1) % n]) for t in range(n)]

    def from_left(x, k):
        turned, at = spread_of(x, k, x[0].shape[0])
        n = len(x)
        return [jnp.where(at >= k, turned[t], turned[t - 1]) for t in range(n)]

    def read(f, r, h):
        return [f[pl.ds(r, h), t * LANES : (t + 1) * LANES] for t in range(count_tiles)]

    def write(f, r, x):
        for t, v in enumerate(x):
            f[pl.ds(r, v.shape[0]), t * LANES : (t + 1) * LANES] = v

    every = range(count_tiles)

    def first_step(r, h, n_before):
        s, s_next = read(S, r, h), read(S, r + h, HALO)
        m = read(M, r, h)
        wet = [v + v for v in m]
        e = from_right([v * w for v, w in zip(read(E, r, h), wet)], 1)
        n0 = [v * w for v, w in zip(read(N, r, h), wet)]
        m_next = read(M, r + h, HALO)
        n_next = [v * (w + w) for v, w in zip(read(N, r + h, HALO), m_next)]
        depth = read(CX, r, h)
        cx = from_right(depth, 1)
        cy = [below(v, w, 1) for v, w in zip(depth, read(CX, r + h, HALO))]
        n = [below(v, w, 1) for v, w in zip(n0, n_next)]
        s_right = from_right(s, 2)
        e = [e[t] + cx[t] * (s_right[t] - s[t]) for t in every]
        n = [n[t] + cy[t] * (below(s[t], s_next[t], 2) - s[t]) for t in every]
        e_left = from_left(e, 2)
        s = [m[t] * (s[t] + s[t] + ((e[t] - e_left[t]) + (n[t] - above(n_before[t], n[t], 2)))) for t in every]
        for f, x in ((S, s), (E, e), (N, n), (CX, cx), (CY, cy)):
            write(f, r, x)
        return [v[h - HALO :] for v in n]

    def second_step(r, h, n_before):
        s, s_next = read(S, r, h), read(S, r + h, HALO)
        e, n, m, cx, cy = (read(f, r, h) for f in (E, N, M, CX, CY))
        s_right = from_right(s, 2)
        e = [e[t] + cx[t] * (s_right[t] - s[t]) for t in every]
        n = [n[t] + cy[t] * (below(s[t], s_next[t], 2) - s[t]) for t in every]
        e_left = from_left(e, 2)
        s = [s[t] + m[t] * ((e[t] - e_left[t]) + (n[t] - above(n_before[t], n[t], 2))) for t in every]
        for f, x in ((S, s), (E, e), (N, n)):
            write(f, r, x)
        return [v[h - HALO :] for v in n]

    within = (lax.broadcasted_iota(jnp.int32, (HALO, LANES), 0).astype(F32) + 0.5) / SPACING
    lower = [spline_weight(within + 1.5 - m) for m in range(4)]
    upper = [spline_weight(within + 1.0 - m) for m in range(4)]
    mine_only = range(tiles)

    def last_step(k, h, carry):
        n_before, sums = carry
        r = HALO + k
        s, s_next = read(S, r, h), read(S, r + h, HALO)
        e, n, m, cx, cy = (read(f, r, h) for f in (E, N, M, CX, CY))
        s_right = from_right(s, 2)
        e = [e[t] + cx[t] * (s_right[t] - s[t]) for t in every]
        n = [n[t] + cy[t] * (below(s[t], s_next[t], 2) - s[t]) for t in mine_only]
        e_left, e_own = from_left(e, 2), from_left(e, 1)
        s = [s[t] + m[t] * ((e[t] - e_left[t]) + (n[t] - above(n_before[t], n[t], 2))) for t in mine_only]
        write(s_out, k, s)
        write(e_out, k, e_own[:tiles])
        write(n_out, k, [above(n_before[t], n[t], 1) for t in mine_only])
        sums = [list(x) for x in sums]
        for q in range(h // SPACING):
            done = []
            for t in mine_only:
                low = s[t][q * SPACING : q * SPACING + HALO]
                up = s[t][q * SPACING + HALO : (q + 1) * SPACING]
                a = [low * w for w in lower]
                b = [up * w for w in upper]
                c = sums[t]
                done.append(jnp.sum(c[0] + a[0], axis=0, keepdims=True))
                sums[t] = [c[1] + (a[1] + b[0]), c[2] + (a[2] + b[1]), c[3] + (a[3] + b[2]), b[3]]
            R[pl.ds(k // SPACING + q, 1), :] = jnp.concatenate(done, axis=1)
        return [v[h - HALO :] for v in n], sums

    zero = [jnp.zeros((HALO, LANES), F32) for _ in every]
    first_step(0, tall, zero)
    second_step(0, tall, zero)
    n_before = []
    for t in mine_only:
        span = slice(t * LANES, (t + 1) * LANES)
        s = S[0:HALO, span]
        n_before.append(N[0:HALO, span] + CY[0:HALO, span] * (below(s, S[HALO : 2 * HALO, span], 2) - s))
    carry = (n_before, [[jnp.zeros((HALO, LANES), F32)] * 4 for _ in mine_only])

    carry = last_step(0, rows, carry)
    for k in range(4):
        tail = [jnp.sum(carry[1][t][k], axis=0, keepdims=True) for t in mine_only]
        R[rows // SPACING + k : rows // SPACING + k + 1, :] = jnp.concatenate(tail, axis=1)

    points = R.shape[0]
    stacked = jnp.concatenate([R[:, t * LANES : (t + 1) * LANES] for t in range(tiles)], axis=0)
    spread = jnp.dot(stacked, column_weight, precision=lax.Precision.HIGHEST, preferred_element_type=F32)
    own = spread[0:points]
    for t in range(1, tiles):
        own = own + right(spread[t * points : (t + 1) * points], 8 * t)
    PART[...] = own

    top, bottom = pl.ds(0, HALO), pl.ds(points - HALO, HALO)
    cross = [
        (PART.at[bottom], fold.at[0, top], NORTH),
        (PART.at[top], fold.at[1, top], SOUTH),
        (PART, fold.at[2], EAST),
        (PART, fold.at[3], WEST),
        (PART.at[bottom], fold.at[4, top], NE),
        (PART.at[bottom], fold.at[5, top], NW),
        (PART.at[top], fold.at[6, top], SE),
        (PART.at[top], fold.at[7, top], SW),
    ]
    cross = messages(cross, len(rim) + len(side))
    start(cross)
    points_load.wait()
    finish(cross)

    row = lax.broadcasted_iota(jnp.int32, (HALO, LANES), 0)
    lane = lanes_of((points, LANES))

    def with_rows(middle, south, north):
        south = jnp.where((row == 2) | (row == 3), south, 0.0)
        north = jnp.where(row < 2, north, 0.0)
        return jnp.concatenate(
            [middle[:HALO] + south, middle[HALO : points - HALO], middle[points - HALO :] + north], axis=0
        )

    mine = with_rows(own, fold[0, 0:HALO], fold[1, 0:HALO])
    west = with_rows(fold[2], fold[4, 0:HALO], fold[6, 0:HALO])
    east = with_rows(fold[3], fold[5, 0:HALO], fold[7, 0:HALO])
    half = cols // SPACING
    west = left(west, half)
    east = right(east, half)
    mine = mine + jnp.where((lane == 2) | (lane == 3), west, 0.0)
    mine = mine + jnp.where((lane == half) | (lane == half + 1), east, 0.0)
    inside = mine[2 : 2 + rows // SPACING, 2 : 2 + half]
    grad[...] = inside * active[...].astype(F32) / SPACING


def deliver(*refs):
    sem = refs[8]
    copies = [pltpu.make_async_copy(refs[k], refs[4 + k], sem.at[k]) for k in range(4)]
    for copy in copies:
        copy.start()
    for copy in copies:
        copy.wait()


def local(surface_adjoint, east_adjoint, north_adjoint, water_depth, wet_mask, control_active):
    rows, cols = surface_adjoint.shape
    points = rows // SPACING + 4
    points = (points + 7) // 8 * 8
    tall, wide = rows + 2 * HALO, cols + LANES
    field = pltpu.VMEM((tall + HALO, wide), F32)
    quarter = rows // 4
    whole = pl.BlockSpec(memory_space=pltpu.VMEM)
    in_hbm = pl.BlockSpec(memory_space=pltpu.HBM)
    shape = jax.ShapeDtypeStruct((rows, cols), F32)
    hold = lambda x: pltpu.with_memory_space_constraint(x, pltpu.HBM)
    s, e, n, g = pl.pallas_call(
        kernel,
        out_shape=(shape, shape, shape, jax.ShapeDtypeStruct(control_active.shape, F32)),
        in_specs=[in_hbm] * 6,
        out_specs=(whole,) * 4,
        scratch_shapes=[
            field, field, field, field,
            field, field,
            pltpu.VMEM((rows, cols), jnp.int32),
            pltpu.VMEM((points, cols), F32),
            pltpu.VMEM((points, LANES), F32),
            pltpu.VMEM(control_active.shape, jnp.int32),
            pltpu.VMEM((quarter, LANES), F32),
            pltpu.VMEM((quarter, LANES), F32),
            pltpu.VMEM((quarter, LANES), F32),
            pltpu.VMEM((quarter, LANES), F32),
            pltpu.VMEM((4, HALO, LANES), F32),
            pltpu.VMEM((8, points, LANES), F32),
            pltpu.SemaphoreType.DMA((26,)),
            pltpu.SemaphoreType.DMA((22,)),
            pltpu.SemaphoreType.DMA((22,)),
        ],
        compiler_params=pltpu.CompilerParams(
            collective_id=0, has_side_effects=True, vmem_limit_bytes=32 * 1024 * 1024
        ),
    )(hold(surface_adjoint), hold(east_adjoint), hold(north_adjoint), hold(water_depth), hold(wet_mask), hold(control_active))
    return pl.pallas_call(
        deliver,
        out_shape=(shape, shape, shape, jax.ShapeDtypeStruct(control_active.shape, F32)),
        in_specs=[whole] * 4,
        out_specs=(in_hbm,) * 4,
        scratch_shapes=[pltpu.SemaphoreType.DMA((4,))],
    )(*[pltpu.with_memory_space_constraint(x, pltpu.VMEM) for x in (s, e, n, g)])


def solution(mesh):
    spec = P("lat", "lon")
    return jax.shard_map(
        local, mesh=mesh, in_specs=(spec,) * 6, out_specs=(spec,) * 4, check_vma=False
    )
```

```python
import jax
import jax.numpy as jnp
from jax import lax
from jax.experimental import pallas as pl
from jax.experimental.pallas import tpu as pltpu
from jax.sharding import PartitionSpec as P

SPACING = 16
LANES = 128
HALO = 8
STEPS = 3
F32 = jnp.float32

SOUTH, NORTH, WEST, EAST = (-1, 0), (1, 0), (0, -1), (0, 1)
SW, SE, NW, NE = (-1, -1), (-1, 1), (1, -1), (1, 1)
NEIGHBOURS = (SOUTH, NORTH, WEST, EAST, SW, SE, NW, NE)


def spline_weight(arg):
    mag = jnp.abs(arg)
    inner = 2.0 / 3.0 - mag * mag + 0.5 * mag * mag * mag
    outer = (2.0 - mag) * (2.0 - mag) * (2.0 - mag) / 6.0
    return jnp.where(mag < 1.0, inner, jnp.where(mag < 2.0, outer, 0.0 * mag))


def lanes_of(shape):
    return lax.broadcasted_iota(jnp.int32, shape, 1)


def below(x, following, k):
    return jnp.concatenate([x, following], axis=0)[k : k + x.shape[0]]


def above(preceding, x, k):
    return jnp.concatenate([preceding, x], axis=0)[HALO - k : HALO - k + x.shape[0]]


def turn(x, k):
    return pltpu.roll(x, k % LANES, axis=1) if k % LANES else x


def from_right(x, k):
    turned = [turn(v, -k) for v in x]
    if len(x) == 1:
        return turned
    at = lanes_of(x[0].shape)
    return [jnp.where(at < LANES - k, turned[t], turned[(t + 1) % len(x)]) for t in range(len(x))]


def from_left(x, k):
    turned = [turn(v, k) for v in x]
    if len(x) == 1:
        return turned
    at = lanes_of(x[0].shape)
    return [jnp.where(at >= k, turned[t], turned[t - 1]) for t in range(len(x))]


def up(x, k):
    none = jnp.zeros((HALO, LANES), F32)
    return [below(v, none, k) for v in x]


def down(x, k):
    none = jnp.zeros((HALO, LANES), F32)
    return [above(none, v, k) for v in x]


def change(s, e, n, cx, cy):
    s_right, s_up = from_right(s, 2), up(s, 2)
    e = [v + c * (r - o) for v, c, r, o in zip(e, cx, s_right, s)]
    n = [v + c * (r - o) for v, c, r, o in zip(n, cy, s_up, s)]
    flow = [(v - l) + (w - d) for v, l, w, d in zip(e, from_left(e, 2), n, down(n, 2))]
    return flow, e, n


def first_step(s, e, n, depth, m):
    wet = [v + v for v in m]
    e = from_right([v * w for v, w in zip(e, wet)], 1)
    n = up([v * w for v, w in zip(n, wet)], 1)
    cx, cy = from_right(depth, 1), up(depth, 1)
    flow, e, n = change(s, e, n, cx, cy)
    s = [w * (v + v + f) for w, v, f in zip(m, s, flow)]
    return s, e, n, cx, cy


def next_step(s, e, n, cx, cy, m):
    flow, e, n = change(s, e, n, cx, cy)
    return [v + w * f for v, w, f in zip(s, m, flow)], e, n


def march(s, e, n, depth):
    m = [jnp.where(v > 0.0, 0.5, 0.0) for v in depth]
    s, e, n, cx, cy = first_step(s, e, n, depth, m)
    for step in range(STEPS - 1):
        s, e, n = next_step(s, e, n, cx, cy, m)
    return s, from_left(e, 1), down(n, 1)


def kernel(
    s_in, e_in, n_in, d_in, w_in, a_in,
    s_out, e_out, n_out, grad,
    S, E, N, D, W, CY, M, R, PART, active,
    TOP, BOT, Z, pack_w, pack_e, got_w, got_e, corner, fold,
    load_sem, send_sem, recv_sem,
):
    rows, cols = s_out.shape
    tiles = cols // LANES
    quarter = rows // 4
    edge = 2 * HALO
    nlat, nlon = lax.axis_size("lat"), lax.axis_size("lon")
    lat, lon = lax.axis_index("lat"), lax.axis_index("lon")

    def has(offset):
        a, b = lat + offset[0], lon + offset[1]
        return (a >= 0) & (a < nlat) & (b >= 0) & (b < nlon)

    def opposite(offset):
        return (-offset[0], -offset[1])

    barrier = pltpu.get_barrier_semaphore()
    count = jnp.int32(0)
    for offset in NEIGHBOURS:
        count = count + has(offset).astype(jnp.int32)

        @pl.when(has(offset))
        def _(offset=offset):
            pl.semaphore_signal(
                barrier, inc=1,
                device_id={"lat": lat + offset[0], "lon": lon + offset[1]},
                device_id_type=pl.DeviceIdType.MESH,
            )

    regions = (
        (0, rows, 0, LANES),
        (0, rows, cols - LANES, LANES),
        (0, edge, LANES, cols - 2 * LANES),
        (rows - edge, edge, LANES, cols - 2 * LANES),
        (edge, rows - 2 * edge, LANES, cols - 2 * LANES),
    )
    loads = []
    for k, (r, h, c, w) in enumerate(regions):
        for a, (src, dst) in enumerate(((w_in, W), (d_in, D), (e_in, E), (n_in, N), (s_in, S))):
            loads.append(
                pltpu.make_async_copy(
                    src.at[pl.ds(r, h), pl.ds(c, w)],
                    dst.at[pl.ds(r, h), pl.ds(c, w)],
                    load_sem.at[k * 5 + a],
                )
            )
    loads.append(pltpu.make_async_copy(a_in, active, load_sem.at[25]))
    for copy in loads:
        copy.start()

    def messages(items, first):
        made = []
        for k, (src, dst, offset) in enumerate(items):
            made.append((
                pltpu.make_async_remote_copy(
                    src_ref=src, dst_ref=dst,
                    send_sem=send_sem.at[first + k], recv_sem=recv_sem.at[first + k],
                    device_id={"lat": lat + offset[0], "lon": lon + offset[1]},
                    device_id_type=pl.DeviceIdType.MESH,
                ),
                offset,
            ))
        return made

    def start(made):
        for copy, offset in made:
            @pl.when(has(offset))
            def _(copy=copy):
                copy.start()

    def finish(made):
        for copy, offset in made:
            @pl.when(has(opposite(offset)))
            def _(copy=copy):
                copy.wait_recv()

            @pl.when(has(offset))
            def _(copy=copy):
                copy.wait_send()

    every = pl.ds(0, 4)
    body = pl.ds(0, cols)
    halos = messages([
        (TOP.at[every, pl.ds(HALO, HALO), body], BOT.at[every, pl.ds(edge, HALO), body], SOUTH),
        (BOT.at[every, pl.ds(HALO, HALO), body], TOP.at[every, pl.ds(0, HALO), body], NORTH),
        (pack_w, got_e, WEST),
        (pack_e, got_w, EAST),
        (pack_w.at[pl.ds(0, HALO)], corner.at[3], SW),
        (pack_e.at[pl.ds(0, HALO)], corner.at[2], SE),
        (pack_w.at[pl.ds(quarter - HALO, HALO)], corner.at[1], NW),
        (pack_e.at[pl.ds(quarter - HALO, HALO)], corner.at[0], NE),
    ], 0)

    @pl.when(lat == 0)
    def _():
        TOP[:, 0:HALO, 0:cols] = jnp.zeros((4, HALO, cols), F32)
        fold[0] = jnp.zeros_like(fold[0])

    @pl.when(lat == nlat - 1)
    def _():
        BOT[:, edge : edge + HALO, 0:cols] = jnp.zeros((4, HALO, cols), F32)
        fold[1] = jnp.zeros_like(fold[1])

    for pack, offset, k in ((got_w, WEST, 2), (got_e, EAST, 3)):
        @pl.when(jnp.logical_not(has(offset)))
        def _(pack=pack, k=k):
            pack[...] = jnp.zeros_like(pack)
            fold[k] = jnp.zeros_like(fold[k])

    for k, offset in enumerate((SW, SE, NW, NE)):
        @pl.when(jnp.logical_not(has(offset)))
        def _(k=k):
            corner[k] = jnp.zeros_like(corner[k])
            fold[4 + k] = jnp.zeros_like(fold[4 + k])

    R[...] = jnp.zeros_like(R)

    def span(t):
        return slice(t * LANES, (t + 1) * LANES)

    def cell(f, r, h, t):
        return f[r : r + h, span(t)]

    def depth_of(r, h, t):
        return cell(D, r, h, t) * (0.5 * cell(W, r, h, t).astype(F32))

    for copy in loads[:20]:
        copy.wait()

    lane = lanes_of((quarter, LANES))
    far = tiles - 1
    sides = {}
    for t in (0, far):
        sides[t] = [cell(f, 0, rows, t) for f in (S, E, N)] + [depth_of(0, rows, t)]
    for pack, t, extra in ((pack_w, 0, 0), (pack_e, far, 1)):
        total = jnp.zeros((quarter, LANES), F32)
        for a in range(4):
            for b in range(4):
                g = 4 * b + a
                piece = turn(sides[t][a][b * quarter : (b + 1) * quarter], 8 * (g + extra))
                total = jnp.where((lane >= 8 * g) & (lane < 8 * g + 8), piece, total)
        pack[...] = total
    for a, f in enumerate((S, E, N, None)):
        for t in range(tiles):
            for buffer, to, r in ((TOP, HALO, 0), (BOT, 0, rows - edge)):
                v = depth_of(r, edge, t) if f is None else cell(f, r, edge, t)
                buffer[a, to : to + edge, span(t)] = v

    tall_lane = lanes_of((rows, LANES))
    for a in range(4):
        Z[a] = jnp.where(tall_lane < 56, turn(sides[far][a], 56), jnp.where(tall_lane >= 72, turn(sides[0][a], 72), 0.0))

    for copy in loads[20:]:
        copy.wait()

    def read(f):
        return [cell(f, 0, rows, t) for t in range(tiles)]

    def write(f, x):
        for t, v in enumerate(x):
            f[:, span(t)] = v

    m = [0.5 * v.astype(F32) for v in read(W)]
    depth = [v * w for v, w in zip(read(D), m)]
    s, e, n, cx, cy = first_step(read(S), read(E), read(N), depth, m)
    for f, x in ((S, s), (E, e), (N, n), (D, cx), (CY, cy), (M, m)):
        write(f, x)

    pl.semaphore_wait(barrier, count)
    start(halos)

    for step in range(STEPS - 2):
        s, e, n = next_step(*(read(f) for f in (S, E, N, D, CY, M)))
        for f, x in ((S, s), (E, e), (N, n)):
            write(f, x)

    s, e, n = next_step(*(read(f) for f in (S, E, N, D, CY, M)))
    for f, x in ((s_out, s), (e_out, from_left(e, 1)), (n_out, down(n, 1))):
        write(f, x)

    within = (lax.broadcasted_iota(jnp.int32, (HALO, LANES), 0).astype(F32) + 0.5) / SPACING
    lower = [spline_weight(within + 1.5 - k) for k in range(4)]
    upper = [spline_weight(within + 1.0 - k) for k in range(4)]

    def total_of(x):
        return jnp.sum(x, axis=0, keepdims=True)

    def row_sums(v, t):
        none = jnp.zeros((HALO, LANES), F32)
        c = [none] * 4
        cells = rows // SPACING
        for q in range(cells):
            r = q * SPACING
            low, high = v[r : r + HALO], v[r + HALO : r + SPACING]
            a = [none] * 4 if q == 0 else [low * w for w in lower]
            b = [none] * 4 if q == cells - 1 else [high * w for w in upper]
            R[q : q + 1, span(t)] = total_of(c[0] + a[0])
            c = [c[1] + (a[1] + b[0]), c[2] + (a[2] + b[1]), c[3] + (a[3] + b[2]), b[3]]
        for k in range(4):
            R[cells + k : cells + k + 1, span(t)] = total_of(c[k])

    s[0] = jnp.where(tall_lane >= 8, s[0], 0.0)
    s[far] = jnp.where(tall_lane < LANES - 8, s[far], 0.0)
    for t in range(tiles):
        row_sums(s[t], t)

    shape = (LANES, LANES)
    at = lax.broadcasted_iota(jnp.int32, shape, 0)
    point = lanes_of(shape).astype(F32) - 2.0 + 0.5
    column_weight = spline_weight((at.astype(F32) + 0.5) / SPACING - point)
    strip_column = jnp.where(at < 64, at + (cols - 56), at - 72)
    strip_weight = spline_weight((strip_column.astype(F32) + 0.5) / SPACING - point)
    strip_weight = jnp.where(((at >= 48) & (at < 56)) | ((at >= 72) & (at < 80)), strip_weight, 0.0)

    finish(halos)

    def ring(east, west, g):
        x = lanes_of(east.shape)
        return jnp.where(x < 8, turn(east, -8 * g), jnp.where(x >= LANES - 8, turn(west, -8 * (g + 1)), 0.0))

    edges = []
    for buffer in (TOP, BOT):
        fields = []
        for a in range(4):
            if buffer is TOP:
                parts = [ring(corner[1], corner[0], 12 + a), ring(got_e[0:edge], got_w[0:edge], a)]
            else:
                last = slice(quarter - edge, quarter)
                parts = [ring(got_e[last], got_w[last], 12 + a), ring(corner[3], corner[2], a)]
            fields.append([buffer[a, :, span(t)] for t in range(tiles)] + [jnp.concatenate(parts, axis=0)])
        edges.append(march(*fields))

    fields = []
    for a in range(4):
        parts = []
        for b in range(4):
            g = 4 * b + a
            own = Z[a, b * quarter : (b + 1) * quarter]
            own = jnp.where((lane >= 56) & (lane < 64), turn(got_e[...], 56 - 8 * g), own)
            parts.append(jnp.where((lane >= 64) & (lane < 72), turn(got_w[...], 64 - 8 * g), own))
        fields.append([jnp.concatenate(parts, axis=0)])
    strip = march(*fields)

    middle = slice(HALO, rows - HALO)
    for f, z, south, north in zip((s_out, e_out, n_out), strip, *edges):
        x = lanes_of((rows - 2 * HALO, LANES))
        f[middle, span(0)] = jnp.where(x < 8, turn(z[0][middle], -72), f[middle, span(0)])
        f[middle, span(far)] = jnp.where(x >= LANES - 8, turn(z[0][middle], 72), f[middle, span(far)])
        for t in range(tiles):
            f[0:HALO, span(t)] = south[t][HALO:edge]
            f[rows - HALO : rows, span(t)] = north[t][HALO:edge]

    row_sums(strip[0][0], tiles)
    cells = rows // SPACING
    for t in range(tiles):
        south, north = edges[0][0][t][HALO:edge], edges[1][0][t][HALO:edge]
        for k in range(4):
            R[k : k + 1, span(t)] += total_of(south * lower[k])
            R[cells + k : cells + k + 1, span(t)] += total_of(north * upper[k])

    points = R.shape[0]

    def dot(x, w):
        return jnp.dot(x, w, precision=lax.Precision.HIGHEST, preferred_element_type=F32)

    spread = dot(jnp.concatenate([R[:, span(t)] for t in range(tiles)], axis=0), column_weight)
    own = dot(R[:, span(tiles)], strip_weight)
    for t in range(tiles):
        own = own + turn(spread[t * points : (t + 1) * points], 8 * t)
    PART[...] = own

    top, bottom = pl.ds(0, HALO), pl.ds(points - HALO, HALO)
    cross = [
        (PART.at[bottom], fold.at[0, top], NORTH),
        (PART.at[top], fold.at[1, top], SOUTH),
        (PART, fold.at[2], EAST),
        (PART, fold.at[3], WEST),
        (PART.at[bottom], fold.at[4, top], NE),
        (PART.at[bottom], fold.at[5, top], NW),
        (PART.at[top], fold.at[6, top], SE),
        (PART.at[top], fold.at[7, top], SW),
    ]
    cross = messages(cross, len(halos))
    start(cross)
    finish(cross)

    row = lax.broadcasted_iota(jnp.int32, (HALO, LANES), 0)
    lane = lanes_of((points, LANES))

    def with_rows(middle, south, north):
        south = jnp.where((row == 2) | (row == 3), south, 0.0)
        north = jnp.where(row < 2, north, 0.0)
        return jnp.concatenate(
            [middle[:HALO] + south, middle[HALO : points - HALO], middle[points - HALO :] + north], axis=0
        )

    mine = with_rows(own, fold[0, 0:HALO], fold[1, 0:HALO])
    west = with_rows(fold[2], fold[4, 0:HALO], fold[6, 0:HALO])
    east = with_rows(fold[3], fold[5, 0:HALO], fold[7, 0:HALO])
    half = cols // SPACING
    west = turn(west, -half)
    east = turn(east, half)
    mine = mine + jnp.where((lane == 2) | (lane == 3), west, 0.0)
    mine = mine + jnp.where((lane == half) | (lane == half + 1), east, 0.0)
    inside = mine[2 : 2 + rows // SPACING, 2 : 2 + half]
    grad[...] = inside * active[...].astype(F32) / SPACING


def deliver(*refs):
    sem = refs[8]
    copies = [pltpu.make_async_copy(refs[k], refs[4 + k], sem.at[k]) for k in range(4)]
    for copy in copies:
        copy.start()
    for copy in copies:
        copy.wait()


def local(surface_adjoint, east_adjoint, north_adjoint, water_depth, wet_mask, control_active):
    rows, cols = surface_adjoint.shape
    points = rows // SPACING + 4
    points = (points + 7) // 8 * 8
    field = pltpu.VMEM((rows, cols), F32)
    rim = pltpu.VMEM((4, 3 * HALO, cols), F32)
    pack = pltpu.VMEM((rows // 4, LANES), F32)
    whole = pl.BlockSpec(memory_space=pltpu.VMEM)
    in_hbm = pl.BlockSpec(memory_space=pltpu.HBM)
    shape = jax.ShapeDtypeStruct((rows, cols), F32)
    hold = lambda x: pltpu.with_memory_space_constraint(x, pltpu.HBM)
    s, e, n, g = pl.pallas_call(
        kernel,
        out_shape=(shape, shape, shape, jax.ShapeDtypeStruct(control_active.shape, F32)),
        in_specs=[in_hbm] * 6,
        out_specs=(whole,) * 4,
        scratch_shapes=[
            field, field, field, field,
            pltpu.VMEM((rows, cols), jnp.int32),
            field, field,
            pltpu.VMEM((points, cols + LANES), F32),
            pltpu.VMEM((points, LANES), F32),
            pltpu.VMEM(control_active.shape, jnp.int32),
            rim, rim,
            pltpu.VMEM((4, rows, LANES), F32),
            pack, pack, pack, pack,
            pltpu.VMEM((4, HALO, LANES), F32),
            pltpu.VMEM((8, points, LANES), F32),
            pltpu.SemaphoreType.DMA((26,)),
            pltpu.SemaphoreType.DMA((16,)),
            pltpu.SemaphoreType.DMA((16,)),
        ],
        compiler_params=pltpu.CompilerParams(
            collective_id=0, has_side_effects=True, vmem_limit_bytes=32 * 1024 * 1024
        ),
    )(hold(surface_adjoint), hold(east_adjoint), hold(north_adjoint), hold(water_depth), hold(wet_mask), hold(control_active))
    return pl.pallas_call(
        deliver,
        out_shape=(shape, shape, shape, jax.ShapeDtypeStruct(control_active.shape, F32)),
        in_specs=[whole] * 4,
        out_specs=(in_hbm,) * 4,
        scratch_shapes=[pltpu.SemaphoreType.DMA((4,))],
    )(*[pltpu.with_memory_space_constraint(x, pltpu.VMEM) for x in (s, e, n, g)])


def solution(mesh):
    spec = P("lat", "lon")
    return jax.shard_map(
        local, mesh=mesh, in_specs=(spec,) * 6, out_specs=(spec,) * 4, check_vma=False
    )
```

```python
import jax
import jax.numpy as jnp
from jax import lax
from jax.experimental import pallas as pl
from jax.experimental.pallas import tpu as pltpu
from jax.sharding import PartitionSpec as P

SPACING = 16
LANES = 128
HALO = 8
WIDE = 32
STEPS = 3
F32 = jnp.float32

SOUTH, NORTH, WEST, EAST = (-1, 0), (1, 0), (0, -1), (0, 1)
SW, SE, NW, NE = (-1, -1), (-1, 1), (1, -1), (1, 1)
NEIGHBOURS = (SOUTH, NORTH, WEST, EAST, SW, SE, NW, NE)


def spline_weight(arg):
    mag = jnp.abs(arg)
    inner = 2.0 / 3.0 - mag * mag + 0.5 * mag * mag * mag
    outer = (2.0 - mag) * (2.0 - mag) * (2.0 - mag) / 6.0
    return jnp.where(mag < 1.0, inner, jnp.where(mag < 2.0, outer, 0.0 * mag))


def lanes_of(shape):
    return lax.broadcasted_iota(jnp.int32, shape, 1)


def below(x, following, k):
    return jnp.concatenate([x, following], axis=0)[k : k + x.shape[0]]


def above(preceding, x, k):
    return jnp.concatenate([preceding, x], axis=0)[HALO - k : HALO - k + x.shape[0]]


def turn(x, k):
    return pltpu.roll(x, k % LANES, axis=1) if k % LANES else x


def from_right(x, k):
    turned = [turn(v, -k) for v in x]
    if len(x) == 1:
        return turned
    at = lanes_of(x[0].shape)
    return [jnp.where(at < LANES - k, turned[t], turned[(t + 1) % len(x)]) for t in range(len(x))]


def from_left(x, k):
    turned = [turn(v, k) for v in x]
    if len(x) == 1:
        return turned
    at = lanes_of(x[0].shape)
    return [jnp.where(at >= k, turned[t], turned[t - 1]) for t in range(len(x))]


def up(x, k):
    none = jnp.zeros((HALO, LANES), F32)
    return [below(v, none, k) for v in x]


def down(x, k):
    none = jnp.zeros((HALO, LANES), F32)
    return [above(none, v, k) for v in x]


def change(s, e, n, cx, cy):
    s_right, s_up = from_right(s, 2), up(s, 2)
    e = [v + c * (r - o) for v, c, r, o in zip(e, cx, s_right, s)]
    n = [v + c * (r - o) for v, c, r, o in zip(n, cy, s_up, s)]
    flow = [(v - l) + (w - d) for v, l, w, d in zip(e, from_left(e, 2), n, down(n, 2))]
    return flow, e, n


def first_step(s, e, n, depth, m):
    wet = [v + v for v in m]
    e = from_right([v * w for v, w in zip(e, wet)], 1)
    n = up([v * w for v, w in zip(n, wet)], 1)
    cx, cy = from_right(depth, 1), up(depth, 1)
    flow, e, n = change(s, e, n, cx, cy)
    s = [w * (v + v + f) for w, v, f in zip(m, s, flow)]
    return s, e, n, cx, cy


def next_step(s, e, n, cx, cy, m):
    flow, e, n = change(s, e, n, cx, cy)
    return [v + w * f for v, w, f in zip(s, m, flow)], e, n


def march(s, e, n, depth):
    m = [jnp.where(v > 0.0, 0.5, 0.0) for v in depth]
    s, e, n, cx, cy = first_step(s, e, n, depth, m)
    for step in range(STEPS - 1):
        s, e, n = next_step(s, e, n, cx, cy, m)
    return s, from_left(e, 1), down(n, 1)


def kernel(
    s_in, e_in, n_in, d_in, w_in, a_in,
    s_out, e_out, n_out, grad,
    S, E, N, D, W, CY, M, R, PART, active,
    TOP, BOT, Z, pack_w, pack_e, got_w, got_e, corner, fold,
    load_sem, send_sem, recv_sem,
):
    rows, cols = s_out.shape
    tiles = cols // LANES
    edge = 2 * HALO
    nlat, nlon = lax.axis_size("lat"), lax.axis_size("lon")
    lat, lon = lax.axis_index("lat"), lax.axis_index("lon")

    def has(offset):
        a, b = lat + offset[0], lon + offset[1]
        return (a >= 0) & (a < nlat) & (b >= 0) & (b < nlon)

    def opposite(offset):
        return (-offset[0], -offset[1])

    barrier = pltpu.get_barrier_semaphore()
    count = jnp.int32(0)
    for offset in NEIGHBOURS:
        count = count + has(offset).astype(jnp.int32)

        @pl.when(has(offset))
        def _(offset=offset):
            pl.semaphore_signal(
                barrier, inc=1,
                device_id={"lat": lat + offset[0], "lon": lon + offset[1]},
                device_id_type=pl.DeviceIdType.MESH,
            )

    regions = (
        (0, rows, 0, LANES),
        (0, rows, cols - LANES, LANES),
        (0, edge, LANES, cols - 2 * LANES),
        (rows - edge, edge, LANES, cols - 2 * LANES),
        (edge, rows - 2 * edge, LANES, cols - 2 * LANES),
    )
    loads = []
    for k, (r, h, c, w) in enumerate(regions):
        for a, (src, dst) in enumerate(((w_in, W), (d_in, D), (e_in, E), (n_in, N), (s_in, S))):
            loads.append(
                pltpu.make_async_copy(
                    src.at[pl.ds(r, h), pl.ds(c, w)],
                    dst.at[pl.ds(r, h), pl.ds(c, w)],
                    load_sem.at[k * 5 + a],
                )
            )
    loads.append(pltpu.make_async_copy(a_in, active, load_sem.at[25]))
    for copy in loads:
        copy.start()

    def messages(items, first):
        made = []
        for k, (src, dst, offset) in enumerate(items):
            made.append((
                pltpu.make_async_remote_copy(
                    src_ref=src, dst_ref=dst,
                    send_sem=send_sem.at[first + k], recv_sem=recv_sem.at[first + k],
                    device_id={"lat": lat + offset[0], "lon": lon + offset[1]},
                    device_id_type=pl.DeviceIdType.MESH,
                ),
                offset,
            ))
        return made

    def start(made):
        for copy, offset in made:
            @pl.when(has(offset))
            def _(copy=copy):
                copy.start()

    def finish(made):
        for copy, offset in made:
            @pl.when(has(opposite(offset)))
            def _(copy=copy):
                copy.wait_recv()

            @pl.when(has(offset))
            def _(copy=copy):
                copy.wait_send()

    every = pl.ds(0, 4)
    body = pl.ds(0, cols)
    halos = messages([
        (TOP.at[every, pl.ds(HALO, HALO), body], BOT.at[every, pl.ds(edge, HALO), body], SOUTH),
        (BOT.at[every, pl.ds(HALO, HALO), body], TOP.at[every, pl.ds(0, HALO), body], NORTH),
        (pack_w, got_e, WEST),
        (pack_e, got_w, EAST),
        (pack_w.at[pl.ds(0, HALO)], corner.at[3], SW),
        (pack_e.at[pl.ds(0, HALO)], corner.at[2], SE),
        (pack_w.at[pl.ds(rows - HALO, HALO)], corner.at[1], NW),
        (pack_e.at[pl.ds(rows - HALO, HALO)], corner.at[0], NE),
    ], 0)

    @pl.when(lat == 0)
    def _():
        TOP[:, 0:HALO, 0:cols] = jnp.zeros((4, HALO, cols), F32)
        fold[0] = jnp.zeros_like(fold[0])

    @pl.when(lat == nlat - 1)
    def _():
        BOT[:, edge : edge + HALO, 0:cols] = jnp.zeros((4, HALO, cols), F32)
        fold[1] = jnp.zeros_like(fold[1])

    for pack, offset in ((got_w, WEST), (got_e, EAST)):
        @pl.when(jnp.logical_not(has(offset)))
        def _(pack=pack):
            pack[...] = jnp.zeros_like(pack)

    for k, offset in enumerate((SW, SE, NW, NE)):
        @pl.when(jnp.logical_not(has(offset)))
        def _(k=k):
            corner[k] = jnp.zeros_like(corner[k])

    R[...] = jnp.zeros_like(R)

    def span(t):
        return slice(t * LANES, (t + 1) * LANES)

    def cell(f, r, h, t):
        return f[r : r + h, span(t)]

    def depth_of(r, h, t):
        return cell(D, r, h, t) * (0.5 * cell(W, r, h, t).astype(F32))

    for copy in loads[:20]:
        copy.wait()

    lane = lanes_of((rows, LANES))
    far = tiles - 1
    sides = {}
    for t in (0, far):
        sides[t] = [cell(f, 0, rows, t) for f in (S, E, N)] + [depth_of(0, rows, t)]

    def pick(x, pieces):
        total = pieces[-1]
        for k in (2, 1, 0):
            total = jnp.where(x < WIDE * (k + 1), pieces[k], total)
        return total

    pack_w[...] = pick(lane, [turn(sides[0][a], WIDE * a) for a in range(4)])
    pack_e[...] = pick(lane, [turn(sides[far][a], WIDE * (a + 1)) for a in range(4)])
    for a, f in enumerate((S, E, N, None)):
        for t in range(tiles):
            for buffer, to, r in ((TOP, HALO, 0), (BOT, 0, rows - edge)):
                v = depth_of(r, edge, t) if f is None else cell(f, r, edge, t)
                buffer[a, to : to + edge, span(t)] = v

    pl.semaphore_wait(barrier, count)
    start(halos)

    for a in range(4):
        Z[a] = jnp.where(lane < 64, turn(sides[far][a], WIDE), turn(sides[0][a], -WIDE))

    for copy in loads[20:]:
        copy.wait()

    def read(f):
        return [cell(f, 0, rows, t) for t in range(tiles)]

    def write(f, x):
        for t, v in enumerate(x):
            f[:, span(t)] = v

    m = [0.5 * v.astype(F32) for v in read(W)]
    depth = [v * w for v, w in zip(read(D), m)]
    s, e, n, cx, cy = first_step(read(S), read(E), read(N), depth, m)
    for f, x in ((S, s), (E, e), (N, n), (D, cx), (CY, cy), (M, m)):
        write(f, x)

    for step in range(STEPS - 2):
        s, e, n = next_step(*(read(f) for f in (S, E, N, D, CY, M)))
        for f, x in ((S, s), (E, e), (N, n)):
            write(f, x)

    s, e, n = next_step(*(read(f) for f in (S, E, N, D, CY, M)))
    for f, x in ((s_out, s), (e_out, from_left(e, 1)), (n_out, down(n, 1))):
        write(f, x)

    within = (lax.broadcasted_iota(jnp.int32, (HALO, LANES), 0).astype(F32) + 0.5) / SPACING
    lower = [spline_weight(within + 1.5 - k) for k in range(4)]
    upper = [spline_weight(within + 1.0 - k) for k in range(4)]

    def total_of(x):
        return jnp.sum(x, axis=0, keepdims=True)

    def row_sums(v, t):
        none = jnp.zeros((HALO, LANES), F32)
        c = [none] * 4
        cells = rows // SPACING
        for q in range(cells):
            r = q * SPACING
            low, high = v[r : r + HALO], v[r + HALO : r + SPACING]
            a = [none] * 4 if q == 0 else [low * w for w in lower]
            b = [none] * 4 if q == cells - 1 else [high * w for w in upper]
            R[q : q + 1, span(t)] = total_of(c[0] + a[0])
            c = [c[1] + (a[1] + b[0]), c[2] + (a[2] + b[1]), c[3] + (a[3] + b[2]), b[3]]
        for k in range(4):
            R[cells + k : cells + k + 1, span(t)] = total_of(c[k])

    s[0] = jnp.where(lane >= 8, s[0], 0.0)
    s[far] = jnp.where(lane < LANES - 8, s[far], 0.0)
    for t in range(tiles):
        row_sums(s[t], t)

    shape = (LANES, LANES)
    at = lax.broadcasted_iota(jnp.int32, shape, 0)
    point = lanes_of(shape).astype(F32) - 2.0 + 0.5
    column_weight = spline_weight((at.astype(F32) + 0.5) / SPACING - point)
    strip_column = jnp.where(at < 64, at + (cols - WIDE), at - 3 * WIDE)
    strip_weight = spline_weight((strip_column.astype(F32) + 0.5) / SPACING - point)
    strip_weight = jnp.where((at >= WIDE - 8) & (at < 3 * WIDE + 8), strip_weight, 0.0)

    finish(halos)

    def ring(east, west, a):
        x = lanes_of(east.shape)
        east, west = turn(east, -WIDE * a), turn(west, -WIDE * (a + 1))
        return jnp.where(x < WIDE, east, jnp.where(x >= LANES - WIDE, west, 0.0))

    edges = []
    for buffer in (TOP, BOT):
        fields = []
        for a in range(4):
            if buffer is TOP:
                parts = [ring(corner[1], corner[0], a), ring(got_e[0:edge], got_w[0:edge], a)]
            else:
                last = slice(rows - edge, rows)
                parts = [ring(got_e[last], got_w[last], a), ring(corner[3], corner[2], a)]
            fields.append([buffer[a, :, span(t)] for t in range(tiles)] + [jnp.concatenate(parts, axis=0)])
        edges.append(march(*fields))

    fields = []
    for a in range(4):
        own = Z[a]
        pieces = [own, turn(got_e[...], WIDE * (1 - a)), turn(got_w[...], WIDE * (2 - a)), own]
        fields.append([pick(lane, pieces)])
    strip = march(*fields)

    middle = slice(HALO, rows - HALO)
    for f, z, south, north in zip((s_out, e_out, n_out), strip, *edges):
        x = lanes_of((rows - 2 * HALO, LANES))
        f[middle, span(0)] = jnp.where(x < 8, turn(z[0][middle], WIDE), f[middle, span(0)])
        f[middle, span(far)] = jnp.where(x >= LANES - 8, turn(z[0][middle], -WIDE), f[middle, span(far)])
        for t in range(tiles):
            f[0:HALO, span(t)] = south[t][HALO:edge]
            f[rows - HALO : rows, span(t)] = north[t][HALO:edge]

    row_sums(strip[0][0], tiles)
    cells = rows // SPACING

    def beyond(x):
        at = lanes_of(x.shape)
        x = jnp.where(at < 64, turn(x, WIDE), turn(x, -WIDE))
        return jnp.where((at >= WIDE) & (at < 3 * WIDE), x, 0.0)

    for t in range(tiles + 1):
        south, north = edges[0][0][t][HALO:edge], edges[1][0][t][HALO:edge]
        if t == tiles:
            south, north = beyond(south), beyond(north)
        for k in range(4):
            R[k : k + 1, span(t)] += total_of(south * lower[k])
            R[cells + k : cells + k + 1, span(t)] += total_of(north * upper[k])

    points = R.shape[0]

    def dot(x, w):
        return jnp.dot(x, w, precision=lax.Precision.HIGHEST, preferred_element_type=F32)

    spread = dot(jnp.concatenate([R[:, span(t)] for t in range(tiles)], axis=0), column_weight)
    own = dot(R[:, span(tiles)], strip_weight)
    for t in range(tiles):
        own = own + turn(spread[t * points : (t + 1) * points], 8 * t)
    PART[...] = own

    top, bottom = pl.ds(0, HALO), pl.ds(points - HALO, HALO)
    cross = messages([
        (PART.at[bottom], fold.at[0], NORTH),
        (PART.at[top], fold.at[1], SOUTH),
    ], len(halos))
    start(cross)
    finish(cross)

    row = lax.broadcasted_iota(jnp.int32, (HALO, LANES), 0)
    mine = jnp.concatenate([
        own[:HALO] + jnp.where((row == 2) | (row == 3), fold[0], 0.0),
        own[HALO : points - HALO],
        own[points - HALO :] + jnp.where(row < 2, fold[1], 0.0),
    ], axis=0)
    inside = mine[2 : 2 + rows // SPACING, 2 : 2 + cols // SPACING]
    grad[...] = inside * active[...].astype(F32) / SPACING


def deliver(*refs):
    sem = refs[8]
    copies = [pltpu.make_async_copy(refs[k], refs[4 + k], sem.at[k]) for k in range(4)]
    for copy in copies:
        copy.start()
    for copy in copies:
        copy.wait()


def local(surface_adjoint, east_adjoint, north_adjoint, water_depth, wet_mask, control_active):
    rows, cols = surface_adjoint.shape
    points = rows // SPACING + 4
    points = (points + 7) // 8 * 8
    field = pltpu.VMEM((rows, cols), F32)
    rim = pltpu.VMEM((4, 3 * HALO, cols), F32)
    pack = pltpu.VMEM((rows, LANES), F32)
    whole = pl.BlockSpec(memory_space=pltpu.VMEM)
    in_hbm = pl.BlockSpec(memory_space=pltpu.HBM)
    shape = jax.ShapeDtypeStruct((rows, cols), F32)
    hold = lambda x: pltpu.with_memory_space_constraint(x, pltpu.HBM)
    s, e, n, g = pl.pallas_call(
        kernel,
        out_shape=(shape, shape, shape, jax.ShapeDtypeStruct(control_active.shape, F32)),
        in_specs=[in_hbm] * 6,
        out_specs=(whole,) * 4,
        scratch_shapes=[
            field, field, field, field,
            pltpu.VMEM((rows, cols), jnp.int32),
            field, field,
            pltpu.VMEM((points, cols + LANES), F32),
            pltpu.VMEM((points, LANES), F32),
            pltpu.VMEM(control_active.shape, jnp.int32),
            rim, rim,
            pltpu.VMEM((4, rows, LANES), F32),
            pack, pack, pack, pack,
            pltpu.VMEM((4, HALO, LANES), F32),
            pltpu.VMEM((2, HALO, LANES), F32),
            pltpu.SemaphoreType.DMA((26,)),
            pltpu.SemaphoreType.DMA((10,)),
            pltpu.SemaphoreType.DMA((10,)),
        ],
        compiler_params=pltpu.CompilerParams(
            collective_id=0, has_side_effects=True, vmem_limit_bytes=32 * 1024 * 1024
        ),
    )(hold(surface_adjoint), hold(east_adjoint), hold(north_adjoint), hold(water_depth), hold(wet_mask), hold(control_active))
    return pl.pallas_call(
        deliver,
        out_shape=(shape, shape, shape, jax.ShapeDtypeStruct(control_active.shape, F32)),
        in_specs=[whole] * 4,
        out_specs=(in_hbm,) * 4,
        scratch_shapes=[pltpu.SemaphoreType.DMA((4,))],
    )(*[pltpu.with_memory_space_constraint(x, pltpu.VMEM) for x in (s, e, n, g)])


def solution(mesh):
    spec = P("lat", "lon")
    return jax.shard_map(
        local, mesh=mesh, in_specs=(spec,) * 6, out_specs=(spec,) * 4, check_vma=False
    )
```

```python
import jax
import jax.numpy as jnp
from jax import lax
from jax.experimental import pallas as pl
from jax.experimental.pallas import tpu as pltpu
from jax.sharding import PartitionSpec as P

SPACING = 16
LANES = 128
HALO = 8
WIDE = 32
CHUNKS = 4
PIECES = 1
STEPS = 3
F32 = jnp.float32

SOUTH, NORTH, WEST, EAST = (-1, 0), (1, 0), (0, -1), (0, 1)
SW, SE, NW, NE = (-1, -1), (-1, 1), (1, -1), (1, 1)
NEIGHBOURS = (SOUTH, NORTH, WEST, EAST, SW, SE, NW, NE)


def spline_weight(arg):
    mag = jnp.abs(arg)
    inner = 2.0 / 3.0 - mag * mag + 0.5 * mag * mag * mag
    outer = (2.0 - mag) * (2.0 - mag) * (2.0 - mag) / 6.0
    return jnp.where(mag < 1.0, inner, jnp.where(mag < 2.0, outer, 0.0 * mag))


def lanes_of(shape):
    return lax.broadcasted_iota(jnp.int32, shape, 1)


def below(x, following, k):
    return jnp.concatenate([x, following], axis=0)[k : k + x.shape[0]]


def above(preceding, x, k):
    return jnp.concatenate([preceding, x], axis=0)[HALO - k : HALO - k + x.shape[0]]


def turn(x, k):
    return pltpu.roll(x, k % LANES, axis=1) if k % LANES else x


def from_right(x, k):
    turned = [turn(v, -k) for v in x]
    if len(x) == 1:
        return turned
    at = lanes_of(x[0].shape)
    return [jnp.where(at < LANES - k, turned[t], turned[(t + 1) % len(x)]) for t in range(len(x))]


def from_left(x, k):
    turned = [turn(v, k) for v in x]
    if len(x) == 1:
        return turned
    at = lanes_of(x[0].shape)
    return [jnp.where(at >= k, turned[t], turned[t - 1]) for t in range(len(x))]


def up(x, k, following=None):
    none = jnp.zeros((HALO, LANES), F32)
    return [below(v, following[i] if following else none, k) for i, v in enumerate(x)]


def down(x, k, preceding=None):
    none = jnp.zeros((HALO, LANES), F32)
    return [above(preceding[i] if preceding else none, v, k) for i, v in enumerate(x)]


def change(s, e, n, cx, cy, s_after=None, n_before=None):
    s_right, s_up = from_right(s, 2), up(s, 2, s_after)
    e = [v + c * (r - o) for v, c, r, o in zip(e, cx, s_right, s)]
    n = [v + c * (r - o) for v, c, r, o in zip(n, cy, s_up, s)]
    flow = [(v - l) + (w - d) for v, l, w, d in zip(e, from_left(e, 2), n, down(n, 2, n_before))]
    return flow, e, n


def first_step(s, e, n, depth, m, after=(None, None, None), n_before=None):
    s_after, n_after, depth_after = after
    wet = [v + v for v in m]
    e = from_right([v * w for v, w in zip(e, wet)], 1)
    n = up([v * w for v, w in zip(n, wet)], 1, n_after)
    cx, cy = from_right(depth, 1), up(depth, 1, depth_after)
    flow, e, n = change(s, e, n, cx, cy, s_after, n_before)
    s = [w * (v + v + f) for w, v, f in zip(m, s, flow)]
    return s, e, n, cx, cy


def next_step(s, e, n, cx, cy, m):
    flow, e, n = change(s, e, n, cx, cy)
    return [v + w * f for v, w, f in zip(s, m, flow)], e, n


def march(s, e, n, depth):
    m = [jnp.where(v > 0.0, 0.5, 0.0) for v in depth]
    s, e, n, cx, cy = first_step(s, e, n, depth, m)
    for step in range(STEPS - 1):
        s, e, n = next_step(s, e, n, cx, cy, m)
    return s, from_left(e, 1), down(n, 1)


def kernel(
    s_in, e_in, n_in, d_in, w_in, a_in,
    s_out, e_out, n_out, grad,
    S, E, N, D, W, CY, M, R, PART, active,
    TOP, BOT, Z, pack_w, pack_e, got_w, got_e, corner, fold,
    load_sem, send_sem, recv_sem,
):
    rows, cols = s_out.shape
    tiles = cols // LANES
    edge = 2 * HALO
    nlat, nlon = lax.axis_size("lat"), lax.axis_size("lon")
    lat, lon = lax.axis_index("lat"), lax.axis_index("lon")

    def has(offset):
        a, b = lat + offset[0], lon + offset[1]
        return (a >= 0) & (a < nlat) & (b >= 0) & (b < nlon)

    def opposite(offset):
        return (-offset[0], -offset[1])

    barrier = pltpu.get_barrier_semaphore()
    count = jnp.int32(0)
    for offset in NEIGHBOURS:
        count = count + has(offset).astype(jnp.int32)

        @pl.when(has(offset))
        def _(offset=offset):
            pl.semaphore_signal(
                barrier, inc=1,
                device_id={"lat": lat + offset[0], "lon": lon + offset[1]},
                device_id_type=pl.DeviceIdType.MESH,
            )

    part = (rows - 2 * edge) // (HALO * CHUNKS) * HALO
    chunks = [(edge + k * part, part) for k in range(CHUNKS - 1)]
    chunks.append((edge + (CHUNKS - 1) * part, rows - 2 * edge - (CHUNKS - 1) * part))
    regions = (
        (0, rows, 0, LANES),
        (0, rows, cols - LANES, LANES),
        (0, edge, LANES, cols - 2 * LANES),
        (rows - edge, edge, LANES, cols - 2 * LANES),
    ) + tuple((r, h, LANES, cols - 2 * LANES) for r, h in chunks)
    loads = []
    for k, (r, h, c, w) in enumerate(regions):
        for a, (src, dst) in enumerate(((w_in, W), (d_in, D), (e_in, E), (n_in, N), (s_in, S))):
            loads.append(
                pltpu.make_async_copy(
                    src.at[pl.ds(r, h), pl.ds(c, w)],
                    dst.at[pl.ds(r, h), pl.ds(c, w)],
                    load_sem.at[k * 5 + a],
                )
            )
    loads.append(pltpu.make_async_copy(a_in, active, load_sem.at[5 * len(regions)]))
    for copy in loads:
        copy.start()

    def messages(items, first):
        made = []
        for k, (src, dst, offset) in enumerate(items):
            made.append((
                pltpu.make_async_remote_copy(
                    src_ref=src, dst_ref=dst,
                    send_sem=send_sem.at[first + k], recv_sem=recv_sem.at[first + k],
                    device_id={"lat": lat + offset[0], "lon": lon + offset[1]},
                    device_id_type=pl.DeviceIdType.MESH,
                ),
                offset,
            ))
        return made

    def start(made):
        for copy, offset in made:
            @pl.when(has(offset))
            def _(copy=copy):
                copy.start()

    def finish(made):
        for copy, offset in made:
            @pl.when(has(opposite(offset)))
            def _(copy=copy):
                copy.wait_recv()

            @pl.when(has(offset))
            def _(copy=copy):
                copy.wait_send()

    every = pl.ds(0, 4)
    body = pl.ds(0, cols)
    halos = messages([
        (TOP.at[every, pl.ds(HALO, HALO), body], BOT.at[every, pl.ds(edge, HALO), body], SOUTH),
        (BOT.at[every, pl.ds(HALO, HALO), body], TOP.at[every, pl.ds(0, HALO), body], NORTH),
        (pack_w, got_e, WEST),
        (pack_e, got_w, EAST),
        (pack_w.at[pl.ds(0, HALO)], corner.at[3], SW),
        (pack_e.at[pl.ds(0, HALO)], corner.at[2], SE),
        (pack_w.at[pl.ds(rows - HALO, HALO)], corner.at[1], NW),
        (pack_e.at[pl.ds(rows - HALO, HALO)], corner.at[0], NE),
    ], 0)

    @pl.when(lat == 0)
    def _():
        TOP[:, 0:HALO, 0:cols] = jnp.zeros((4, HALO, cols), F32)
        fold[0] = jnp.zeros_like(fold[0])

    @pl.when(lat == nlat - 1)
    def _():
        BOT[:, edge : edge + HALO, 0:cols] = jnp.zeros((4, HALO, cols), F32)
        fold[1] = jnp.zeros_like(fold[1])

    for pack, offset in ((got_w, WEST), (got_e, EAST)):
        @pl.when(jnp.logical_not(has(offset)))
        def _(pack=pack):
            pack[...] = jnp.zeros_like(pack)

    for k, offset in enumerate((SW, SE, NW, NE)):
        @pl.when(jnp.logical_not(has(offset)))
        def _(k=k):
            corner[k] = jnp.zeros_like(corner[k])

    R[...] = jnp.zeros_like(R)

    def span(t):
        return slice(t * LANES, (t + 1) * LANES)

    def cell(f, r, h, t):
        return f[r : r + h, span(t)]

    def depth_of(r, h, t):
        return cell(D, r, h, t) * (0.5 * cell(W, r, h, t).astype(F32))

    for copy in loads[:10]:
        copy.wait()

    lane = lanes_of((rows, LANES))
    far = tiles - 1
    sides = {}
    for t in (0, far):
        sides[t] = [cell(f, 0, rows, t) for f in (S, E, N)] + [depth_of(0, rows, t)]

    def pick(x, pieces):
        total = pieces[-1]
        for k in (2, 1, 0):
            total = jnp.where(x < WIDE * (k + 1), pieces[k], total)
        return total

    pack_w[...] = pick(lane, [turn(sides[0][a], WIDE * a) for a in range(4)])
    pack_e[...] = pick(lane, [turn(sides[far][a], WIDE * (a + 1)) for a in range(4)])
    pl.semaphore_wait(barrier, count)
    start(halos[2:])

    for copy in loads[10:20]:
        copy.wait()
    for a, f in enumerate((S, E, N, None)):
        for t in range(tiles):
            for buffer, to, r in ((TOP, HALO, 0), (BOT, 0, rows - edge)):
                v = depth_of(r, edge, t) if f is None else cell(f, r, edge, t)
                buffer[a, to : to + edge, span(t)] = v

    start(halos[:2])

    for a in range(4):
        Z[a] = jnp.where(lane < 64, turn(sides[far][a], WIDE), turn(sides[0][a], -WIDE))

    def read(f, r=0, h=rows):
        return [cell(f, r, h, t) for t in range(tiles)]

    def write(f, x, r=0):
        for t, v in enumerate(x):
            f[r : r + v.shape[0], span(t)] = v

    n_before = None
    begin = 0
    for k, (r, h) in enumerate(chunks):
        for copy in loads[20 + 5 * k : 25 + 5 * k]:
            copy.wait()
        last = k == len(chunks) - 1
        end = rows if last else r + h - HALO
        height = end - begin
        m = [0.5 * v.astype(F32) for v in read(W, begin, height)]
        depth = [v * w for v, w in zip(read(D, begin, height), m)]
        after = (None, None, None)
        if not last:
            half = [0.5 * v.astype(F32) for v in read(W, end, HALO)]
            after = (
                read(S, end, HALO),
                [v * (w + w) for v, w in zip(read(N, end, HALO), half)],
                [v * w for v, w in zip(read(D, end, HALO), half)],
            )
        s, e, n, cx, cy = first_step(
            read(S, begin, height), read(E, begin, height), read(N, begin, height), depth, m, after, n_before
        )
        for f, x in ((S, s), (E, e), (N, n), (D, cx), (CY, cy), (M, m)):
            write(f, x, begin)
        n_before = [v[height - HALO :] for v in n]
        begin = end
    loads[-1].wait()

    for step in range(STEPS - 2):
        s, e, n = next_step(*(read(f) for f in (S, E, N, D, CY, M)))
        for f, x in ((S, s), (E, e), (N, n)):
            write(f, x)

    s, e, n = next_step(*(read(f) for f in (S, E, N, D, CY, M)))
    for f, x in ((s_out, s), (e_out, from_left(e, 1)), (n_out, down(n, 1))):
        write(f, x)

    within = (lax.broadcasted_iota(jnp.int32, (HALO, LANES), 0).astype(F32) + 0.5) / SPACING
    lower = [spline_weight(within + 1.5 - k) for k in range(4)]
    upper = [spline_weight(within + 1.0 - k) for k in range(4)]

    def total_of(x):
        return jnp.sum(x, axis=0, keepdims=True)

    def row_sums(v, t):
        none = jnp.zeros((HALO, LANES), F32)
        c = [none] * 4
        cells = rows // SPACING
        for q in range(cells):
            r = q * SPACING
            low, high = v[r : r + HALO], v[r + HALO : r + SPACING]
            a = [none] * 4 if q == 0 else [low * w for w in lower]
            b = [none] * 4 if q == cells - 1 else [high * w for w in upper]
            R[q : q + 1, span(t)] = total_of(c[0] + a[0])
            c = [c[1] + (a[1] + b[0]), c[2] + (a[2] + b[1]), c[3] + (a[3] + b[2]), b[3]]
        for k in range(4):
            R[cells + k : cells + k + 1, span(t)] = total_of(c[k])

    s[0] = jnp.where(lane >= 8, s[0], 0.0)
    s[far] = jnp.where(lane < LANES - 8, s[far], 0.0)
    for t in range(tiles):
        row_sums(s[t], t)

    shape = (LANES, LANES)
    at = lax.broadcasted_iota(jnp.int32, shape, 0)
    point = lanes_of(shape).astype(F32) - 2.0 + 0.5
    column_weight = spline_weight((at.astype(F32) + 0.5) / SPACING - point)
    strip_column = jnp.where(at < 64, at + (cols - WIDE), at - 3 * WIDE)
    strip_weight = spline_weight((strip_column.astype(F32) + 0.5) / SPACING - point)
    strip_weight = jnp.where((at >= WIDE - 8) & (at < 3 * WIDE + 8), strip_weight, 0.0)

    finish(halos)

    def ring(east, west, a):
        x = lanes_of(east.shape)
        east, west = turn(east, -WIDE * a), turn(west, -WIDE * (a + 1))
        return jnp.where(x < WIDE, east, jnp.where(x >= LANES - WIDE, west, 0.0))

    edges = []
    for buffer in (TOP, BOT):
        fields = []
        for a in range(4):
            if buffer is TOP:
                parts = [ring(corner[1], corner[0], a), ring(got_e[0:edge], got_w[0:edge], a)]
            else:
                last = slice(rows - edge, rows)
                parts = [ring(got_e[last], got_w[last], a), ring(corner[3], corner[2], a)]
            fields.append([buffer[a, :, span(t)] for t in range(tiles)] + [jnp.concatenate(parts, axis=0)])
        edges.append(march(*fields))

    fields = []
    for a in range(4):
        own = Z[a]
        pieces = [own, turn(got_e[...], WIDE * (1 - a)), turn(got_w[...], WIDE * (2 - a)), own]
        fields.append([pick(lane, pieces)])
    strip = march(*fields)

    row_sums(strip[0][0], tiles)
    cells = rows // SPACING

    def beyond(x):
        at = lanes_of(x.shape)
        x = jnp.where(at < 64, turn(x, WIDE), turn(x, -WIDE))
        return jnp.where((at >= WIDE) & (at < 3 * WIDE), x, 0.0)

    for t in range(tiles + 1):
        south, north = edges[0][0][t][HALO:edge], edges[1][0][t][HALO:edge]
        if t == tiles:
            south, north = beyond(south), beyond(north)
        for k in range(4):
            R[k : k + 1, span(t)] += total_of(south * lower[k])
            R[cells + k : cells + k + 1, span(t)] += total_of(north * upper[k])

    points = R.shape[0]

    def dot(x, w):
        return jnp.dot(x, w, precision=lax.Precision.HIGHEST, preferred_element_type=F32)

    spread = dot(jnp.concatenate([R[:, span(t)] for t in range(tiles)], axis=0), column_weight)
    own = dot(R[:, span(tiles)], strip_weight)
    for t in range(tiles):
        own = own + turn(spread[t * points : (t + 1) * points], 8 * t)
    PART[...] = own

    top, bottom = pl.ds(0, HALO), pl.ds(points - HALO, HALO)
    cross = messages([
        (PART.at[bottom], fold.at[0], NORTH),
        (PART.at[top], fold.at[1], SOUTH),
    ], len(halos))
    start(cross)

    middle = slice(HALO, rows - HALO)
    for f, z, south, north in zip((s_out, e_out, n_out), strip, *edges):
        x = lanes_of((rows - 2 * HALO, LANES))
        f[middle, span(0)] = jnp.where(x < 8, turn(z[0][middle], WIDE), f[middle, span(0)])
        f[middle, span(far)] = jnp.where(x >= LANES - 8, turn(z[0][middle], -WIDE), f[middle, span(far)])
        for t in range(tiles):
            f[0:HALO, span(t)] = south[t][HALO:edge]
            f[rows - HALO : rows, span(t)] = north[t][HALO:edge]

    finish(cross)

    row = lax.broadcasted_iota(jnp.int32, (HALO, LANES), 0)
    mine = jnp.concatenate([
        own[:HALO] + jnp.where((row == 2) | (row == 3), fold[0], 0.0),
        own[HALO : points - HALO],
        own[points - HALO :] + jnp.where(row < 2, fold[1], 0.0),
    ], axis=0)
    inside = mine[2 : 2 + rows // SPACING, 2 : 2 + cols // SPACING]
    grad[...] = inside * active[...].astype(F32) / SPACING


def deliver(*refs):
    sem = refs[8]
    copies = []
    for k in range(3):
        rows = refs[k].shape[0] // PIECES
        for p in range(PIECES):
            here = pl.ds(p * rows, rows)
            copies.append(
                pltpu.make_async_copy(refs[k].at[here], refs[4 + k].at[here], sem.at[len(copies)])
            )
    copies.append(pltpu.make_async_copy(refs[3], refs[7], sem.at[len(copies)]))
    for copy in copies:
        copy.start()
    for copy in copies:
        copy.wait()


def local(surface_adjoint, east_adjoint, north_adjoint, water_depth, wet_mask, control_active):
    rows, cols = surface_adjoint.shape
    points = rows // SPACING + 4
    points = (points + 7) // 8 * 8
    field = pltpu.VMEM((rows, cols), F32)
    rim = pltpu.VMEM((4, 3 * HALO, cols), F32)
    pack = pltpu.VMEM((rows, LANES), F32)
    whole = pl.BlockSpec(memory_space=pltpu.VMEM)
    in_hbm = pl.BlockSpec(memory_space=pltpu.HBM)
    shape = jax.ShapeDtypeStruct((rows, cols), F32)
    hold = lambda x: pltpu.with_memory_space_constraint(x, pltpu.HBM)
    s, e, n, g = pl.pallas_call(
        kernel,
        out_shape=(shape, shape, shape, jax.ShapeDtypeStruct(control_active.shape, F32)),
        in_specs=[in_hbm] * 6,
        out_specs=(whole,) * 4,
        scratch_shapes=[
            field, field, field, field,
            pltpu.VMEM((rows, cols), jnp.int32),
            field, field,
            pltpu.VMEM((points, cols + LANES), F32),
            pltpu.VMEM((points, LANES), F32),
            pltpu.VMEM(control_active.shape, jnp.int32),
            rim, rim,
            pltpu.VMEM((4, rows, LANES), F32),
            pack, pack, pack, pack,
            pltpu.VMEM((4, HALO, LANES), F32),
            pltpu.VMEM((2, HALO, LANES), F32),
            pltpu.SemaphoreType.DMA((5 * (4 + CHUNKS) + 1,)),
            pltpu.SemaphoreType.DMA((10,)),
            pltpu.SemaphoreType.DMA((10,)),
        ],
        compiler_params=pltpu.CompilerParams(
            collective_id=0, has_side_effects=True, vmem_limit_bytes=32 * 1024 * 1024
        ),
    )(hold(surface_adjoint), hold(east_adjoint), hold(north_adjoint), hold(water_depth), hold(wet_mask), hold(control_active))
    return pl.pallas_call(
        deliver,
        out_shape=(shape, shape, shape, jax.ShapeDtypeStruct(control_active.shape, F32)),
        in_specs=[whole] * 4,
        out_specs=(in_hbm,) * 4,
        scratch_shapes=[pltpu.SemaphoreType.DMA((3 * PIECES + 1,))],
    )(*[pltpu.with_memory_space_constraint(x, pltpu.VMEM) for x in (s, e, n, g)])


def solution(mesh):
    spec = P("lat", "lon")
    return jax.shard_map(
        local, mesh=mesh, in_specs=(spec,) * 6, out_specs=(spec,) * 4, check_vma=False
    )
```

```python
import jax
import jax.numpy as jnp
from jax import lax
from jax.experimental import pallas as pl
from jax.experimental.pallas import tpu as pltpu
from jax.sharding import PartitionSpec as P

SPACING = 16
LANES = 128
HALO = 8
WIDE = 32
CHUNKS = 4
PIECES = 1
STEPS = 3
F32 = jnp.float32

SOUTH, NORTH, WEST, EAST = (-1, 0), (1, 0), (0, -1), (0, 1)
SW, SE, NW, NE = (-1, -1), (-1, 1), (1, -1), (1, 1)
NEIGHBOURS = (SOUTH, NORTH, WEST, EAST, SW, SE, NW, NE)


def spline_weight(arg):
    mag = jnp.abs(arg)
    inner = 2.0 / 3.0 - mag * mag + 0.5 * mag * mag * mag
    outer = (2.0 - mag) * (2.0 - mag) * (2.0 - mag) / 6.0
    return jnp.where(mag < 1.0, inner, jnp.where(mag < 2.0, outer, 0.0 * mag))


def lanes_of(shape):
    return lax.broadcasted_iota(jnp.int32, shape, 1)


def below(x, following, k):
    return jnp.concatenate([x, following], axis=0)[k : k + x.shape[0]]


def above(preceding, x, k):
    return jnp.concatenate([preceding, x], axis=0)[HALO - k : HALO - k + x.shape[0]]


def turn(x, k):
    return pltpu.roll(x, k % LANES, axis=1) if k % LANES else x


def from_right(x, k):
    turned = [turn(v, -k) for v in x]
    if len(x) == 1:
        return turned
    at = lanes_of(x[0].shape)
    return [jnp.where(at < LANES - k, turned[t], turned[(t + 1) % len(x)]) for t in range(len(x))]


def from_left(x, k):
    turned = [turn(v, k) for v in x]
    if len(x) == 1:
        return turned
    at = lanes_of(x[0].shape)
    return [jnp.where(at >= k, turned[t], turned[t - 1]) for t in range(len(x))]


def up(x, k, following=None):
    none = jnp.zeros((HALO, LANES), F32)
    return [below(v, following[i] if following else none, k) for i, v in enumerate(x)]


def down(x, k, preceding=None):
    none = jnp.zeros((HALO, LANES), F32)
    return [above(preceding[i] if preceding else none, v, k) for i, v in enumerate(x)]


def change(s, e, n, cx, cy, s_after=None, n_before=None):
    s_right, s_up = from_right(s, 2), up(s, 2, s_after)
    e = [v + c * (r - o) for v, c, r, o in zip(e, cx, s_right, s)]
    n = [v + c * (r - o) for v, c, r, o in zip(n, cy, s_up, s)]
    flow = [(v - l) + (w - d) for v, l, w, d in zip(e, from_left(e, 2), n, down(n, 2, n_before))]
    return flow, e, n


def first_step(s, e, n, depth, m, after=(None, None, None), n_before=None):
    s_after, n_after, depth_after = after
    wet = [v + v for v in m]
    e = from_right([v * w for v, w in zip(e, wet)], 1)
    n = up([v * w for v, w in zip(n, wet)], 1, n_after)
    cx, cy = from_right(depth, 1), up(depth, 1, depth_after)
    flow, e, n = change(s, e, n, cx, cy, s_after, n_before)
    s = [w * (v + v + f) for w, v, f in zip(m, s, flow)]
    return s, e, n, cx, cy


def next_step(s, e, n, cx, cy, m):
    flow, e, n = change(s, e, n, cx, cy)
    return [v + w * f for v, w, f in zip(s, m, flow)], e, n


def march(s, e, n, depth):
    m = [jnp.where(v > 0.0, 0.5, 0.0) for v in depth]
    s, e, n, cx, cy = first_step(s, e, n, depth, m)
    for step in range(STEPS - 1):
        s, e, n = next_step(s, e, n, cx, cy, m)
    return s, from_left(e, 1), down(n, 1)


def kernel(
    s_in, e_in, n_in, d_in, w_in, a_in,
    s_out, e_out, n_out, grad,
    S, E, N, D, W, CY, M, R, PART, active,
    TOP, BOT, Z, pack_w, pack_e, got_w, got_e, corner, fold,
    load_sem, send_sem, recv_sem,
):
    rows, cols = s_out.shape
    tiles = cols // LANES
    edge = 2 * HALO
    nlat, nlon = lax.axis_size("lat"), lax.axis_size("lon")
    lat, lon = lax.axis_index("lat"), lax.axis_index("lon")

    def has(offset):
        a, b = lat + offset[0], lon + offset[1]
        return (a >= 0) & (a < nlat) & (b >= 0) & (b < nlon)

    def opposite(offset):
        return (-offset[0], -offset[1])

    barrier = pltpu.get_barrier_semaphore()
    count = jnp.int32(0)
    for offset in NEIGHBOURS:
        count = count + has(offset).astype(jnp.int32)

        @pl.when(has(offset))
        def _(offset=offset):
            pl.semaphore_signal(
                barrier, inc=1,
                device_id={"lat": lat + offset[0], "lon": lon + offset[1]},
                device_id_type=pl.DeviceIdType.MESH,
            )

    part = (rows - 2 * edge) // (HALO * CHUNKS) * HALO
    chunks = [(edge + k * part, part) for k in range(CHUNKS - 1)]
    chunks.append((edge + (CHUNKS - 1) * part, rows - 2 * edge - (CHUNKS - 1) * part))
    regions = (
        (0, rows, 0, LANES),
        (0, rows, cols - LANES, LANES),
        (0, edge, LANES, cols - 2 * LANES),
        (rows - edge, edge, LANES, cols - 2 * LANES),
    ) + tuple((r, h, LANES, cols - 2 * LANES) for r, h in chunks)
    loads = []
    for k, (r, h, c, w) in enumerate(regions):
        for a, (src, dst) in enumerate(((w_in, W), (d_in, D), (e_in, E), (n_in, N), (s_in, S))):
            loads.append(
                pltpu.make_async_copy(
                    src.at[pl.ds(r, h), pl.ds(c, w)],
                    dst.at[pl.ds(r, h), pl.ds(c, w)],
                    load_sem.at[k * 5 + a],
                )
            )
    loads.append(pltpu.make_async_copy(a_in, active, load_sem.at[5 * len(regions)]))
    for copy in loads:
        copy.start()

    def messages(items, first):
        made = []
        for k, (src, dst, offset) in enumerate(items):
            made.append((
                pltpu.make_async_remote_copy(
                    src_ref=src, dst_ref=dst,
                    send_sem=send_sem.at[first + k], recv_sem=recv_sem.at[first + k],
                    device_id={"lat": lat + offset[0], "lon": lon + offset[1]},
                    device_id_type=pl.DeviceIdType.MESH,
                ),
                offset,
            ))
        return made

    def start(made):
        for copy, offset in made:
            @pl.when(has(offset))
            def _(copy=copy):
                copy.start()

    def finish(made):
        for copy, offset in made:
            @pl.when(has(opposite(offset)))
            def _(copy=copy):
                copy.wait_recv()

            @pl.when(has(offset))
            def _(copy=copy):
                copy.wait_send()

    every = pl.ds(0, 4)
    body = pl.ds(0, cols)
    halos = messages([
        (TOP.at[every, pl.ds(HALO, HALO), body], BOT.at[every, pl.ds(edge, HALO), body], SOUTH),
        (BOT.at[every, pl.ds(HALO, HALO), body], TOP.at[every, pl.ds(0, HALO), body], NORTH),
        (pack_w, got_e, WEST),
        (pack_e, got_w, EAST),
        (pack_w.at[pl.ds(0, HALO)], corner.at[3], SW),
        (pack_e.at[pl.ds(0, HALO)], corner.at[2], SE),
        (pack_w.at[pl.ds(rows - HALO, HALO)], corner.at[1], NW),
        (pack_e.at[pl.ds(rows - HALO, HALO)], corner.at[0], NE),
    ], 0)

    @pl.when(lat == 0)
    def _():
        TOP[:, 0:HALO, 0:cols] = jnp.zeros((4, HALO, cols), F32)
        fold[0] = jnp.zeros_like(fold[0])

    @pl.when(lat == nlat - 1)
    def _():
        BOT[:, edge : edge + HALO, 0:cols] = jnp.zeros((4, HALO, cols), F32)
        fold[1] = jnp.zeros_like(fold[1])

    for pack, offset in ((got_w, WEST), (got_e, EAST)):
        @pl.when(jnp.logical_not(has(offset)))
        def _(pack=pack):
            pack[...] = jnp.zeros_like(pack)

    for k, offset in enumerate((SW, SE, NW, NE)):
        @pl.when(jnp.logical_not(has(offset)))
        def _(k=k):
            corner[k] = jnp.zeros_like(corner[k])

    R[...] = jnp.zeros_like(R)

    def span(t):
        return slice(t * LANES, (t + 1) * LANES)

    def cell(f, r, h, t):
        return f[r : r + h, span(t)]

    def depth_of(r, h, t):
        return cell(D, r, h, t) * (0.5 * cell(W, r, h, t).astype(F32))

    for copy in loads[:10]:
        copy.wait()

    lane = lanes_of((rows, LANES))
    far = tiles - 1
    sides = {}
    for t in (0, far):
        sides[t] = [cell(f, 0, rows, t) for f in (S, E, N)] + [depth_of(0, rows, t)]

    def pick(x, pieces):
        total = pieces[-1]
        for k in (2, 1, 0):
            total = jnp.where(x < WIDE * (k + 1), pieces[k], total)
        return total

    pack_w[...] = pick(lane, [turn(sides[0][a], WIDE * a) for a in range(4)])
    pack_e[...] = pick(lane, [turn(sides[far][a], WIDE * (a + 1)) for a in range(4)])
    pl.semaphore_wait(barrier, count)
    start(halos[2:])

    for copy in loads[10:20]:
        copy.wait()
    for a, f in enumerate((S, E, N, None)):
        for t in range(tiles):
            for buffer, to, r in ((TOP, HALO, 0), (BOT, 0, rows - edge)):
                v = depth_of(r, edge, t) if f is None else cell(f, r, edge, t)
                buffer[a, to : to + edge, span(t)] = v

    start(halos[:2])

    for a in range(4):
        Z[a] = jnp.where(lane < 64, turn(sides[far][a], WIDE), turn(sides[0][a], -WIDE))

    def read(f, r=0, h=rows):
        return [cell(f, r, h, t) for t in range(tiles)]

    def write(f, x, r=0):
        for t, v in enumerate(x):
            f[r : r + v.shape[0], span(t)] = v

    n_before = None
    begin = 0
    for k, (r, h) in enumerate(chunks):
        for copy in loads[20 + 5 * k : 25 + 5 * k]:
            copy.wait()
        last = k == len(chunks) - 1
        end = rows if last else r + h - HALO
        height = end - begin
        m = [0.5 * v.astype(F32) for v in read(W, begin, height)]
        depth = [v * w for v, w in zip(read(D, begin, height), m)]
        after = (None, None, None)
        if not last:
            half = [0.5 * v.astype(F32) for v in read(W, end, HALO)]
            after = (
                read(S, end, HALO),
                [v * (w + w) for v, w in zip(read(N, end, HALO), half)],
                [v * w for v, w in zip(read(D, end, HALO), half)],
            )
        s, e, n, cx, cy = first_step(
            read(S, begin, height), read(E, begin, height), read(N, begin, height), depth, m, after, n_before
        )
        for f, x in ((S, s), (E, e), (N, n), (D, cx), (CY, cy), (M, m)):
            write(f, x, begin)
        n_before = [v[height - HALO :] for v in n]
        begin = end
    loads[-1].wait()

    for step in range(STEPS - 2):
        s, e, n = next_step(*(read(f) for f in (S, E, N, D, CY, M)))
        for f, x in ((S, s), (E, e), (N, n)):
            write(f, x)

    s, e, n = next_step(*(read(f) for f in (S, E, N, D, CY, M)))
    for f, x in ((s_out, s), (e_out, from_left(e, 1)), (n_out, down(n, 1))):
        write(f, x)

    within = (lax.broadcasted_iota(jnp.int32, (HALO, LANES), 0).astype(F32) + 0.5) / SPACING
    lower = [spline_weight(within + 1.5 - k) for k in range(4)]
    upper = [spline_weight(within + 1.0 - k) for k in range(4)]

    def total_of(x):
        return jnp.sum(x, axis=0, keepdims=True)

    cells = rows // SPACING

    def row_sums(v, t, whole):
        none = jnp.zeros((HALO, LANES), F32)
        c = [none] * 4
        for q in range(cells):
            r = q * SPACING
            low, high = v[r : r + HALO], v[r + HALO : r + SPACING]
            a = [low * w for w in lower] if whole or q > 0 else [none] * 4
            b = [high * w for w in upper] if whole or q < cells - 1 else [none] * 4
            R[q : q + 1, span(t)] = total_of(c[0] + a[0])
            c = [c[1] + (a[1] + b[0]), c[2] + (a[2] + b[1]), c[3] + (a[3] + b[2]), b[3]]
        for k in range(4):
            R[cells + k : cells + k + 1, span(t)] = total_of(c[k])

    def inner_columns(x):
        at = lanes_of(x[0].shape)
        x[0] = jnp.where(at >= 8, x[0], 0.0)
        x[far] = jnp.where(at < LANES - 8, x[far], 0.0)
        return x

    s = inner_columns(s)
    for t in range(tiles):
        row_sums(s[t], t, False)

    shape = (LANES, LANES)
    at = lax.broadcasted_iota(jnp.int32, shape, 0)
    point = lanes_of(shape).astype(F32) - 2.0 + 0.5
    column_weight = spline_weight((at.astype(F32) + 0.5) / SPACING - point)
    strip_column = jnp.where(at < 64, at + (cols - WIDE), at - 3 * WIDE)
    strip_weight = spline_weight((strip_column.astype(F32) + 0.5) / SPACING - point)
    strip_weight = jnp.where((at >= WIDE - 8) & (at < 3 * WIDE + 8), strip_weight, 0.0)

    def dot(x, w):
        return jnp.dot(x, w, precision=lax.Precision.HIGHEST, preferred_element_type=F32)

    finish(halos[:2])
    edges = [march(*([buffer[a, :, span(t)] for t in range(tiles)] for a in range(4))) for buffer in (TOP, BOT)]
    for f, south, north in zip((s_out, e_out, n_out), *edges):
        for t in range(tiles):
            f[0:HALO, span(t)] = south[t][HALO:edge]
            f[rows - HALO : rows, span(t)] = north[t][HALO:edge]
    south = inner_columns([v[HALO:edge] for v in edges[0][0]])
    north = inner_columns([v[HALO:edge] for v in edges[1][0]])
    for t in range(tiles):
        for k in range(4):
            R[k : k + 1, span(t)] += total_of(south[t] * lower[k])
            R[cells + k : cells + k + 1, span(t)] += total_of(north[t] * upper[k])

    points = R.shape[0]
    spread = dot(jnp.concatenate([R[:, span(t)] for t in range(tiles)], axis=0), column_weight)
    own = spread[0:points]
    for t in range(1, tiles):
        own = own + turn(spread[t * points : (t + 1) * points], 8 * t)

    finish(halos[2:])
    fields = []
    for a in range(4):
        parts = []
        for near, east, west in (
            ([TOP[a, 0:HALO, span(t)] for t in (far, 0)], corner[1], corner[0]),
            (None, got_e[...], got_w[...]),
            ([BOT[a, edge : edge + HALO, span(t)] for t in (far, 0)], corner[3], corner[2]),
        ):
            x = lanes_of(east.shape)
            mine = Z[a] if near is None else jnp.where(x < 64, turn(near[0], WIDE), turn(near[1], -WIDE))
            parts.append(pick(x, [mine, turn(east, WIDE * (1 - a)), turn(west, WIDE * (2 - a)), mine]))
        fields.append([jnp.concatenate(parts, axis=0)])
    strip = [x[0][HALO : HALO + rows] for x in march(*fields)]
    row_sums(strip[0], tiles, True)
    own = own + dot(R[:, span(tiles)], strip_weight)
    PART[...] = own

    top, bottom = pl.ds(0, HALO), pl.ds(points - HALO, HALO)
    cross = messages([
        (PART.at[bottom], fold.at[0], NORTH),
        (PART.at[top], fold.at[1], SOUTH),
    ], len(halos))
    start(cross)

    for f, z in zip((s_out, e_out, n_out), strip):
        f[:, span(0)] = jnp.where(lane < 8, turn(z, WIDE), f[:, span(0)])
        f[:, span(far)] = jnp.where(lane >= LANES - 8, turn(z, -WIDE), f[:, span(far)])
    finish(cross)

    row = lax.broadcasted_iota(jnp.int32, (HALO, LANES), 0)
    mine = jnp.concatenate([
        own[:HALO] + jnp.where((row == 2) | (row == 3), fold[0], 0.0),
        own[HALO : points - HALO],
        own[points - HALO :] + jnp.where(row < 2, fold[1], 0.0),
    ], axis=0)
    inside = mine[2 : 2 + rows // SPACING, 2 : 2 + cols // SPACING]
    grad[...] = inside * active[...].astype(F32) / SPACING


def deliver(*refs):
    sem = refs[8]
    copies = []
    for k in range(3):
        rows = refs[k].shape[0] // PIECES
        for p in range(PIECES):
            here = pl.ds(p * rows, rows)
            copies.append(
                pltpu.make_async_copy(refs[k].at[here], refs[4 + k].at[here], sem.at[len(copies)])
            )
    copies.append(pltpu.make_async_copy(refs[3], refs[7], sem.at[len(copies)]))
    for copy in copies:
        copy.start()
    for copy in copies:
        copy.wait()


def local(surface_adjoint, east_adjoint, north_adjoint, water_depth, wet_mask, control_active):
    rows, cols = surface_adjoint.shape
    points = rows // SPACING + 4
    points = (points + 7) // 8 * 8
    field = pltpu.VMEM((rows, cols), F32)
    rim = pltpu.VMEM((4, 3 * HALO, cols), F32)
    pack = pltpu.VMEM((rows, LANES), F32)
    whole = pl.BlockSpec(memory_space=pltpu.VMEM)
    in_hbm = pl.BlockSpec(memory_space=pltpu.HBM)
    shape = jax.ShapeDtypeStruct((rows, cols), F32)
    hold = lambda x: pltpu.with_memory_space_constraint(x, pltpu.HBM)
    s, e, n, g = pl.pallas_call(
        kernel,
        out_shape=(shape, shape, shape, jax.ShapeDtypeStruct(control_active.shape, F32)),
        in_specs=[in_hbm] * 6,
        out_specs=(whole,) * 4,
        scratch_shapes=[
            field, field, field, field,
            pltpu.VMEM((rows, cols), jnp.int32),
            field, field,
            pltpu.VMEM((points, cols + LANES), F32),
            pltpu.VMEM((points, LANES), F32),
            pltpu.VMEM(control_active.shape, jnp.int32),
            rim, rim,
            pltpu.VMEM((4, rows, LANES), F32),
            pack, pack, pack, pack,
            pltpu.VMEM((4, HALO, LANES), F32),
            pltpu.VMEM((2, HALO, LANES), F32),
            pltpu.SemaphoreType.DMA((5 * (4 + CHUNKS) + 1,)),
            pltpu.SemaphoreType.DMA((10,)),
            pltpu.SemaphoreType.DMA((10,)),
        ],
        compiler_params=pltpu.CompilerParams(
            collective_id=0, has_side_effects=True, vmem_limit_bytes=32 * 1024 * 1024
        ),
    )(hold(surface_adjoint), hold(east_adjoint), hold(north_adjoint), hold(water_depth), hold(wet_mask), hold(control_active))
    return pl.pallas_call(
        deliver,
        out_shape=(shape, shape, shape, jax.ShapeDtypeStruct(control_active.shape, F32)),
        in_specs=[whole] * 4,
        out_specs=(in_hbm,) * 4,
        scratch_shapes=[pltpu.SemaphoreType.DMA((3 * PIECES + 1,))],
    )(*[pltpu.with_memory_space_constraint(x, pltpu.VMEM) for x in (s, e, n, g)])


def solution(mesh):
    spec = P("lat", "lon")
    return jax.shard_map(
        local, mesh=mesh, in_specs=(spec,) * 6, out_specs=(spec,) * 4, check_vma=False
    )
```

```python
import jax
import jax.numpy as jnp
from jax import lax
from jax.experimental import pallas as pl
from jax.experimental.pallas import tpu as pltpu
from jax.sharding import PartitionSpec as P

SPACING = 16
LANES = 128
HALO = 8
WIDE = 32
CHUNKS = 4
PIECES = 1
STEPS = 3
F32 = jnp.float32

SOUTH, NORTH, WEST, EAST = (-1, 0), (1, 0), (0, -1), (0, 1)
SW, SE, NW, NE = (-1, -1), (-1, 1), (1, -1), (1, 1)
NEIGHBOURS = (SOUTH, NORTH, WEST, EAST, SW, SE, NW, NE)


def spline_weight(arg):
    mag = jnp.abs(arg)
    inner = 2.0 / 3.0 - mag * mag + 0.5 * mag * mag * mag
    outer = (2.0 - mag) * (2.0 - mag) * (2.0 - mag) / 6.0
    return jnp.where(mag < 1.0, inner, jnp.where(mag < 2.0, outer, 0.0 * mag))


def lanes_of(shape):
    return lax.broadcasted_iota(jnp.int32, shape, 1)


def below(x, following, k):
    return jnp.concatenate([x, following], axis=0)[k : k + x.shape[0]]


def above(preceding, x, k):
    return jnp.concatenate([preceding, x], axis=0)[HALO - k : HALO - k + x.shape[0]]


def turn(x, k):
    return pltpu.roll(x, k % LANES, axis=1) if k % LANES else x


def from_right(x, k):
    turned = [turn(v, -k) for v in x]
    if len(x) == 1:
        return turned
    at = lanes_of(x[0].shape)
    return [jnp.where(at < LANES - k, turned[t], turned[(t + 1) % len(x)]) for t in range(len(x))]


def from_left(x, k):
    turned = [turn(v, k) for v in x]
    if len(x) == 1:
        return turned
    at = lanes_of(x[0].shape)
    return [jnp.where(at >= k, turned[t], turned[t - 1]) for t in range(len(x))]


def up(x, k, following=None):
    none = jnp.zeros((HALO, LANES), F32)
    return [below(v, following[i] if following else none, k) for i, v in enumerate(x)]


def down(x, k, preceding=None):
    none = jnp.zeros((HALO, LANES), F32)
    return [above(preceding[i] if preceding else none, v, k) for i, v in enumerate(x)]


def change(s, e, n, cx, cy, s_after=None, n_before=None):
    s_right, s_up = from_right(s, 2), up(s, 2, s_after)
    e = [v + c * (r - o) for v, c, r, o in zip(e, cx, s_right, s)]
    n = [v + c * (r - o) for v, c, r, o in zip(n, cy, s_up, s)]
    flow = [(v - l) + (w - d) for v, l, w, d in zip(e, from_left(e, 2), n, down(n, 2, n_before))]
    return flow, e, n


def first_step(s, e, n, depth, m, after=(None, None, None), n_before=None):
    s_after, n_after, depth_after = after
    wet = [v + v for v in m]
    e = from_right([v * w for v, w in zip(e, wet)], 1)
    n = up([v * w for v, w in zip(n, wet)], 1, n_after)
    cx, cy = from_right(depth, 1), up(depth, 1, depth_after)
    flow, e, n = change(s, e, n, cx, cy, s_after, n_before)
    s = [w * (v + v + f) for w, v, f in zip(m, s, flow)]
    return s, e, n, cx, cy


def next_step(s, e, n, cx, cy, m):
    flow, e, n = change(s, e, n, cx, cy)
    return [v + w * f for v, w, f in zip(s, m, flow)], e, n


def march(s, e, n, depth):
    m = [jnp.where(v > 0.0, 0.5, 0.0) for v in depth]
    s, e, n, cx, cy = first_step(s, e, n, depth, m)
    for step in range(STEPS - 1):
        s, e, n = next_step(s, e, n, cx, cy, m)
    return s, from_left(e, 1), down(n, 1)


def kernel(
    s_in, e_in, n_in, d_in, w_in, a_in,
    s_out, e_out, n_out, grad,
    S, E, N, D, W, CY, M, R, PART, active,
    TOP, BOT, Z, pack_w, pack_e, got_w, got_e, corner, side, fold, RE,
    load_sem, send_sem, recv_sem,
):
    rows, cols = s_out.shape
    tiles = cols // LANES
    edge = 2 * HALO
    nlat, nlon = lax.axis_size("lat"), lax.axis_size("lon")
    lat, lon = lax.axis_index("lat"), lax.axis_index("lon")

    def has(offset):
        a, b = lat + offset[0], lon + offset[1]
        return (a >= 0) & (a < nlat) & (b >= 0) & (b < nlon)

    def opposite(offset):
        return (-offset[0], -offset[1])

    barrier = pltpu.get_barrier_semaphore()
    count = jnp.int32(0)
    for offset in NEIGHBOURS:
        count = count + has(offset).astype(jnp.int32)

        @pl.when(has(offset))
        def _(offset=offset):
            pl.semaphore_signal(
                barrier, inc=1,
                device_id={"lat": lat + offset[0], "lon": lon + offset[1]},
                device_id_type=pl.DeviceIdType.MESH,
            )

    part = (rows - 2 * edge) // (HALO * CHUNKS) * HALO
    chunks = [(edge + k * part, part) for k in range(CHUNKS - 1)]
    chunks.append((edge + (CHUNKS - 1) * part, rows - 2 * edge - (CHUNKS - 1) * part))
    regions = (
        (0, rows, 0, LANES),
        (0, rows, cols - LANES, LANES),
        (0, edge, LANES, cols - 2 * LANES),
        (rows - edge, edge, LANES, cols - 2 * LANES),
    ) + tuple((r, h, LANES, cols - 2 * LANES) for r, h in chunks)
    loads = []
    for k, (r, h, c, w) in enumerate(regions):
        for a, (src, dst) in enumerate(((w_in, W), (d_in, D), (e_in, E), (n_in, N), (s_in, S))):
            loads.append(
                pltpu.make_async_copy(
                    src.at[pl.ds(r, h), pl.ds(c, w)],
                    dst.at[pl.ds(r, h), pl.ds(c, w)],
                    load_sem.at[k * 5 + a],
                )
            )
    loads.append(pltpu.make_async_copy(a_in, active, load_sem.at[5 * len(regions)]))
    for copy in loads:
        copy.start()

    def messages(items, first):
        made = []
        for k, (src, dst, offset) in enumerate(items):
            made.append((
                pltpu.make_async_remote_copy(
                    src_ref=src, dst_ref=dst,
                    send_sem=send_sem.at[first + k], recv_sem=recv_sem.at[first + k],
                    device_id={"lat": lat + offset[0], "lon": lon + offset[1]},
                    device_id_type=pl.DeviceIdType.MESH,
                ),
                offset,
            ))
        return made

    def start(made):
        for copy, offset in made:
            @pl.when(has(offset))
            def _(copy=copy):
                copy.start()

    def finish(made):
        for copy, offset in made:
            @pl.when(has(opposite(offset)))
            def _(copy=copy):
                copy.wait_recv()

            @pl.when(has(offset))
            def _(copy=copy):
                copy.wait_send()

    every = pl.ds(0, 4)
    body = pl.ds(0, cols)
    first, final = pl.ds(0, WIDE), pl.ds(rows - WIDE, WIDE)
    halos = messages([
        (TOP.at[every, pl.ds(edge, edge), body], BOT.at[every, pl.ds(edge, edge), body], SOUTH),
        (BOT.at[every, pl.ds(0, edge), body], TOP.at[every, pl.ds(0, edge), body], NORTH),
        (pack_w, got_e, WEST),
        (pack_e, got_w, EAST),
        (pack_w.at[first], corner.at[3], SW),
        (pack_e.at[first], corner.at[2], SE),
        (pack_w.at[final], corner.at[1], NW),
        (pack_e.at[final], corner.at[0], NE),
        (pack_w.at[first], side.at[2], SOUTH),
        (pack_e.at[first], side.at[3], SOUTH),
        (pack_w.at[final], side.at[0], NORTH),
        (pack_e.at[final], side.at[1], NORTH),
    ], 0)

    @pl.when(lat == 0)
    def _():
        TOP[:, 0:edge, 0:cols] = jnp.zeros((4, edge, cols), F32)
        side[0:2] = jnp.zeros_like(side[0:2])
        fold[0] = jnp.zeros_like(fold[0])

    @pl.when(lat == nlat - 1)
    def _():
        BOT[:, edge : 2 * edge, 0:cols] = jnp.zeros((4, edge, cols), F32)
        side[2:4] = jnp.zeros_like(side[2:4])
        fold[1] = jnp.zeros_like(fold[1])

    for pack, offset in ((got_w, WEST), (got_e, EAST)):
        @pl.when(jnp.logical_not(has(offset)))
        def _(pack=pack):
            pack[...] = jnp.zeros_like(pack)

    for k, offset in enumerate((SW, SE, NW, NE)):
        @pl.when(jnp.logical_not(has(offset)))
        def _(k=k):
            corner[k] = jnp.zeros_like(corner[k])

    R[...] = jnp.zeros_like(R)

    def span(t):
        return slice(t * LANES, (t + 1) * LANES)

    def cell(f, r, h, t):
        return f[r : r + h, span(t)]

    def depth_of(r, h, t):
        return cell(D, r, h, t) * (0.5 * cell(W, r, h, t).astype(F32))

    for copy in loads[:10]:
        copy.wait()

    lane = lanes_of((rows, LANES))
    far = tiles - 1
    sides = {}
    for t in (0, far):
        sides[t] = [cell(f, 0, rows, t) for f in (S, E, N)] + [depth_of(0, rows, t)]

    def pick(x, pieces):
        total = pieces[-1]
        for k in (2, 1, 0):
            total = jnp.where(x < WIDE * (k + 1), pieces[k], total)
        return total

    pack_w[...] = pick(lane, [turn(sides[0][a], WIDE * a) for a in range(4)])
    pack_e[...] = pick(lane, [turn(sides[far][a], WIDE * (a + 1)) for a in range(4)])
    pl.semaphore_wait(barrier, count)
    start(halos[2:])

    for copy in loads[10:20]:
        copy.wait()
    for a, f in enumerate((S, E, N, None)):
        for t in range(tiles):
            for buffer, to, r in ((TOP, edge, 0), (BOT, 0, rows - edge)):
                v = depth_of(r, edge, t) if f is None else cell(f, r, edge, t)
                buffer[a, to : to + edge, span(t)] = v

    start(halos[:2])

    for a in range(4):
        Z[a] = jnp.where(lane < 64, turn(sides[far][a], WIDE), turn(sides[0][a], -WIDE))

    def read(f, r=0, h=rows):
        return [cell(f, r, h, t) for t in range(tiles)]

    def write(f, x, r=0):
        for t, v in enumerate(x):
            f[r : r + v.shape[0], span(t)] = v

    n_before = None
    begin = 0
    for k, (r, h) in enumerate(chunks):
        for copy in loads[20 + 5 * k : 25 + 5 * k]:
            copy.wait()
        last = k == len(chunks) - 1
        end = rows if last else r + h - HALO
        height = end - begin
        m = [0.5 * v.astype(F32) for v in read(W, begin, height)]
        depth = [v * w for v, w in zip(read(D, begin, height), m)]
        after = (None, None, None)
        if not last:
            half = [0.5 * v.astype(F32) for v in read(W, end, HALO)]
            after = (
                read(S, end, HALO),
                [v * (w + w) for v, w in zip(read(N, end, HALO), half)],
                [v * w for v, w in zip(read(D, end, HALO), half)],
            )
        s, e, n, cx, cy = first_step(
            read(S, begin, height), read(E, begin, height), read(N, begin, height), depth, m, after, n_before
        )
        for f, x in ((S, s), (E, e), (N, n), (D, cx), (CY, cy), (M, m)):
            write(f, x, begin)
        n_before = [v[height - HALO :] for v in n]
        begin = end
    loads[-1].wait()

    for step in range(STEPS - 2):
        s, e, n = next_step(*(read(f) for f in (S, E, N, D, CY, M)))
        for f, x in ((S, s), (E, e), (N, n)):
            write(f, x)

    s, e, n = next_step(*(read(f) for f in (S, E, N, D, CY, M)))
    for f, x in ((s_out, s), (e_out, from_left(e, 1)), (n_out, down(n, 1))):
        write(f, x)

    within = (lax.broadcasted_iota(jnp.int32, (HALO, LANES), 0).astype(F32) + 0.5) / SPACING
    lower = [spline_weight(within + 1.5 - k) for k in range(4)]
    upper = [spline_weight(within + 1.0 - k) for k in range(4)]

    def total_of(x):
        return jnp.sum(x, axis=0, keepdims=True)

    cells = rows // SPACING

    def row_sums(v, t):
        none = jnp.zeros((HALO, LANES), F32)
        c = [none] * 4
        for q in range(cells):
            r = q * SPACING
            low, high = v[r : r + HALO], v[r + HALO : r + SPACING]
            a = [low * w for w in lower] if q > 0 else [none] * 4
            b = [high * w for w in upper] if q < cells - 1 else [none] * 4
            R[q : q + 1, span(t)] = total_of(c[0] + a[0])
            c = [c[1] + (a[1] + b[0]), c[2] + (a[2] + b[1]), c[3] + (a[3] + b[2]), b[3]]
        for k in range(4):
            R[cells + k : cells + k + 1, span(t)] = total_of(c[k])

    def strip_sums(v):
        none = jnp.zeros((HALO, LANES), F32)
        c = [none] * 4
        for q in range(-2, cells + 2):
            r = WIDE + q * SPACING
            low, high = v[r : r + HALO], v[r + HALO : r + SPACING]
            a = [low * w for w in lower] if q > -2 else [none] * 4
            b = [high * w for w in upper] if q < cells + 1 else [none] * 4
            if q >= 2:
                R[q : q + 1, span(tiles)] = total_of(c[0] + a[0])
            c = [c[1] + (a[1] + b[0]), c[2] + (a[2] + b[1]), c[3] + (a[3] + b[2]), b[3]]

    def inner_columns(x):
        at = lanes_of(x[0].shape)
        x[0] = jnp.where(at >= 8, x[0], 0.0)
        x[far] = jnp.where(at < LANES - 8, x[far], 0.0)
        return x

    s = inner_columns(s)
    for t in range(tiles):
        row_sums(s[t], t)

    shape = (LANES, LANES)
    at = lax.broadcasted_iota(jnp.int32, shape, 0)
    point = lanes_of(shape).astype(F32) - 2.0 + 0.5
    column_weight = spline_weight((at.astype(F32) + 0.5) / SPACING - point)
    strip_column = jnp.where(at < 64, at + (cols - WIDE), at - 3 * WIDE)
    strip_weight = spline_weight((strip_column.astype(F32) + 0.5) / SPACING - point)
    strip_weight = jnp.where((at >= WIDE - 8) & (at < 3 * WIDE + 8), strip_weight, 0.0)

    def dot(x, w):
        return jnp.dot(x, w, precision=lax.Precision.HIGHEST, preferred_element_type=F32)

    def along(f):
        h = f.shape[0]
        spread = dot(jnp.concatenate([f[:, span(t)] for t in range(tiles)], axis=0), column_weight)
        total = spread[0:h]
        for t in range(1, tiles):
            total = total + turn(spread[t * h : (t + 1) * h], 8 * t)
        return total

    points = R.shape[0]
    own = along(R)
    PART[...] = own
    top, bottom = pl.ds(0, HALO), pl.ds(points - HALO, HALO)
    cross = messages([
        (PART.at[bottom], fold.at[0], NORTH),
        (PART.at[top], fold.at[1], SOUTH),
    ], len(halos))
    start(cross)

    finish(halos[:2])
    edges = [march(*([buffer[a, :, span(t)] for t in range(tiles)] for a in range(4))) for buffer in (TOP, BOT)]
    for f, south, north in zip((s_out, e_out, n_out), *edges):
        for t in range(tiles):
            f[0:HALO, span(t)] = south[t][edge : edge + HALO]
            f[rows - HALO : rows, span(t)] = north[t][HALO:edge]
    south = inner_columns([v[HALO : edge + HALO] for v in edges[0][0]])
    north = inner_columns([v[HALO : edge + HALO] for v in edges[1][0]])
    for t in range(tiles):
        for k in range(4):
            RE[k : k + 1, span(t)] = total_of(south[t][:HALO] * upper[k] + south[t][HALO:] * lower[k])
            RE[4 + k : 5 + k, span(t)] = total_of(north[t][:HALO] * upper[k] + north[t][HALO:] * lower[k])
    more = along(RE)
    none = jnp.zeros((4, LANES), F32)
    own = jnp.concatenate([
        own[:HALO] + jnp.concatenate([more[0:4], none], axis=0),
        own[HALO : points - HALO],
        own[points - HALO :] + jnp.concatenate([more[4:8], none], axis=0),
    ], axis=0)

    finish(halos[2:])
    fields = []
    for a in range(4):
        parts = []
        for last, east, west, near in (
            (side[1], corner[1], corner[0], side[0]),
            (None, got_e[...], got_w[...], None),
            (side[3], corner[3], corner[2], side[2]),
        ):
            x = lanes_of(east.shape)
            last = Z[a] if last is None else turn(last, -WIDE * a)
            near = Z[a] if near is None else turn(near, WIDE * (3 - a))
            parts.append(pick(x, [last, turn(east, WIDE * (1 - a)), turn(west, WIDE * (2 - a)), near]))
        fields.append([jnp.concatenate(parts, axis=0)])
    strip = [x[0] for x in march(*fields)]
    strip_sums(strip[0])
    strip = [x[WIDE : WIDE + rows] for x in strip]
    own = own + dot(R[:, span(tiles)], strip_weight)

    for f, z in zip((s_out, e_out, n_out), strip):
        f[:, span(0)] = jnp.where(lane < 8, turn(z, WIDE), f[:, span(0)])
        f[:, span(far)] = jnp.where(lane >= LANES - 8, turn(z, -WIDE), f[:, span(far)])
    finish(cross)

    row = lax.broadcasted_iota(jnp.int32, (HALO, LANES), 0)
    mine = jnp.concatenate([
        own[:HALO] + jnp.where((row == 2) | (row == 3), fold[0], 0.0),
        own[HALO : points - HALO],
        own[points - HALO :] + jnp.where(row < 2, fold[1], 0.0),
    ], axis=0)
    inside = mine[2 : 2 + rows // SPACING, 2 : 2 + cols // SPACING]
    grad[...] = inside * active[...].astype(F32) / SPACING


def deliver(*refs):
    sem = refs[8]
    copies = []
    for k in range(3):
        rows = refs[k].shape[0] // PIECES
        for p in range(PIECES):
            here = pl.ds(p * rows, rows)
            copies.append(
                pltpu.make_async_copy(refs[k].at[here], refs[4 + k].at[here], sem.at[len(copies)])
            )
    copies.append(pltpu.make_async_copy(refs[3], refs[7], sem.at[len(copies)]))
    for copy in copies:
        copy.start()
    for copy in copies:
        copy.wait()


def local(surface_adjoint, east_adjoint, north_adjoint, water_depth, wet_mask, control_active):
    rows, cols = surface_adjoint.shape
    points = rows // SPACING + 4
    points = (points + 7) // 8 * 8
    field = pltpu.VMEM((rows, cols), F32)
    rim = pltpu.VMEM((4, 4 * HALO, cols), F32)
    pack = pltpu.VMEM((rows, LANES), F32)
    whole = pl.BlockSpec(memory_space=pltpu.VMEM)
    in_hbm = pl.BlockSpec(memory_space=pltpu.HBM)
    shape = jax.ShapeDtypeStruct((rows, cols), F32)
    hold = lambda x: pltpu.with_memory_space_constraint(x, pltpu.HBM)
    s, e, n, g = pl.pallas_call(
        kernel,
        out_shape=(shape, shape, shape, jax.ShapeDtypeStruct(control_active.shape, F32)),
        in_specs=[in_hbm] * 6,
        out_specs=(whole,) * 4,
        scratch_shapes=[
            field, field, field, field,
            pltpu.VMEM((rows, cols), jnp.int32),
            field, field,
            pltpu.VMEM((points, cols + LANES), F32),
            pltpu.VMEM((points, LANES), F32),
            pltpu.VMEM(control_active.shape, jnp.int32),
            rim, rim,
            pltpu.VMEM((4, rows, LANES), F32),
            pack, pack, pack, pack,
            pltpu.VMEM((4, WIDE, LANES), F32),
            pltpu.VMEM((4, WIDE, LANES), F32),
            pltpu.VMEM((2, HALO, LANES), F32),
            pltpu.VMEM((HALO, cols), F32),
            pltpu.SemaphoreType.DMA((5 * (4 + CHUNKS) + 1,)),
            pltpu.SemaphoreType.DMA((14,)),
            pltpu.SemaphoreType.DMA((14,)),
        ],
        compiler_params=pltpu.CompilerParams(
            collective_id=0, has_side_effects=True, vmem_limit_bytes=32 * 1024 * 1024
        ),
    )(hold(surface_adjoint), hold(east_adjoint), hold(north_adjoint), hold(water_depth), hold(wet_mask), hold(control_active))
    return pl.pallas_call(
        deliver,
        out_shape=(shape, shape, shape, jax.ShapeDtypeStruct(control_active.shape, F32)),
        in_specs=[whole] * 4,
        out_specs=(in_hbm,) * 4,
        scratch_shapes=[pltpu.SemaphoreType.DMA((3 * PIECES + 1,))],
    )(*[pltpu.with_memory_space_constraint(x, pltpu.VMEM) for x in (s, e, n, g)])


def solution(mesh):
    spec = P("lat", "lon")
    return jax.shard_map(
        local, mesh=mesh, in_specs=(spec,) * 6, out_specs=(spec,) * 4, check_vma=False
    )
```

```python
import jax
import jax.numpy as jnp
from jax import lax
from jax.experimental import pallas as pl
from jax.experimental.pallas import tpu as pltpu
from jax.sharding import PartitionSpec as P

SPACING = 16
LANES = 128
HALO = 8
WIDE = 32
CHUNKS = 4
PIECES = 1
STEPS = 3
F32 = jnp.float32

SOUTH, NORTH, WEST, EAST = (-1, 0), (1, 0), (0, -1), (0, 1)
SW, SE, NW, NE = (-1, -1), (-1, 1), (1, -1), (1, 1)
NEIGHBOURS = (SOUTH, NORTH, WEST, EAST, SW, SE, NW, NE)


def spline_weight(arg):
    mag = jnp.abs(arg)
    inner = 2.0 / 3.0 - mag * mag + 0.5 * mag * mag * mag
    outer = (2.0 - mag) * (2.0 - mag) * (2.0 - mag) / 6.0
    return jnp.where(mag < 1.0, inner, jnp.where(mag < 2.0, outer, 0.0 * mag))


def lanes_of(shape):
    return lax.broadcasted_iota(jnp.int32, shape, 1)


def below(x, following, k):
    return jnp.concatenate([x, following], axis=0)[k : k + x.shape[0]]


def above(preceding, x, k):
    return jnp.concatenate([preceding, x], axis=0)[HALO - k : HALO - k + x.shape[0]]


def turn(x, k):
    return pltpu.roll(x, k % LANES, axis=1) if k % LANES else x


def from_right(x, k):
    turned = [turn(v, -k) for v in x]
    if len(x) == 1:
        return turned
    at = lanes_of(x[0].shape)
    return [jnp.where(at < LANES - k, turned[t], turned[(t + 1) % len(x)]) for t in range(len(x))]


def from_left(x, k):
    turned = [turn(v, k) for v in x]
    if len(x) == 1:
        return turned
    at = lanes_of(x[0].shape)
    return [jnp.where(at >= k, turned[t], turned[t - 1]) for t in range(len(x))]


def up(x, k, following=None):
    none = jnp.zeros((HALO, LANES), F32)
    return [below(v, following[i] if following else none, k) for i, v in enumerate(x)]


def down(x, k, preceding=None):
    none = jnp.zeros((HALO, LANES), F32)
    return [above(preceding[i] if preceding else none, v, k) for i, v in enumerate(x)]


def change(s, e, n, cx, cy, s_after=None, n_before=None):
    s_right, s_up = from_right(s, 2), up(s, 2, s_after)
    e = [v + c * (r - o) for v, c, r, o in zip(e, cx, s_right, s)]
    n = [v + c * (r - o) for v, c, r, o in zip(n, cy, s_up, s)]
    flow = [(v - l) + (w - d) for v, l, w, d in zip(e, from_left(e, 2), n, down(n, 2, n_before))]
    return flow, e, n


def first_step(s, e, n, depth, m, after=(None, None, None), n_before=None):
    s_after, n_after, depth_after = after
    wet = [v + v for v in m]
    e = from_right([v * w for v, w in zip(e, wet)], 1)
    n = up([v * w for v, w in zip(n, wet)], 1, n_after)
    cx, cy = from_right(depth, 1), up(depth, 1, depth_after)
    flow, e, n = change(s, e, n, cx, cy, s_after, n_before)
    s = [w * (v + v + f) for w, v, f in zip(m, s, flow)]
    return s, e, n, cx, cy


def next_step(s, e, n, cx, cy, m):
    flow, e, n = change(s, e, n, cx, cy)
    return [v + w * f for v, w, f in zip(s, m, flow)], e, n


def march(s, e, n, depth):
    m = [jnp.where(v > 0.0, 0.5, 0.0) for v in depth]
    s, e, n, cx, cy = first_step(s, e, n, depth, m)
    for step in range(STEPS - 1):
        s, e, n = next_step(s, e, n, cx, cy, m)
    return s, from_left(e, 1), down(n, 1)


def kernel(
    s_in, e_in, n_in, d_in, w_in, a_in,
    s_out, e_out, n_out, grad,
    S, E, N, D, W, CY, M, R, PART, active,
    TOP, BOT, Z, pack_w, pack_e, got_w, got_e, corner, side, fold, RE,
    load_sem, send_sem, recv_sem,
):
    rows, cols = s_out.shape
    tiles = cols // LANES
    edge = 2 * HALO
    nlat, nlon = lax.axis_size("lat"), lax.axis_size("lon")
    lat, lon = lax.axis_index("lat"), lax.axis_index("lon")

    def has(offset):
        a, b = lat + offset[0], lon + offset[1]
        return (a >= 0) & (a < nlat) & (b >= 0) & (b < nlon)

    def opposite(offset):
        return (-offset[0], -offset[1])

    barrier = pltpu.get_barrier_semaphore()
    count = jnp.int32(0)
    for offset in NEIGHBOURS:
        count = count + has(offset).astype(jnp.int32)

        @pl.when(has(offset))
        def _(offset=offset):
            pl.semaphore_signal(
                barrier, inc=1,
                device_id={"lat": lat + offset[0], "lon": lon + offset[1]},
                device_id_type=pl.DeviceIdType.MESH,
            )

    part = (rows - 2 * edge) // (HALO * CHUNKS) * HALO
    chunks = [(edge + k * part, part) for k in range(CHUNKS - 1)]
    chunks.append((edge + (CHUNKS - 1) * part, rows - 2 * edge - (CHUNKS - 1) * part))
    regions = (
        (0, rows, 0, LANES),
        (0, rows, cols - LANES, LANES),
        (0, edge, LANES, cols - 2 * LANES),
        (rows - edge, edge, LANES, cols - 2 * LANES),
    ) + tuple((r, h, LANES, cols - 2 * LANES) for r, h in chunks)
    loads = []
    for k, (r, h, c, w) in enumerate(regions):
        for a, (src, dst) in enumerate(((w_in, W), (d_in, D), (e_in, E), (n_in, N), (s_in, S))):
            loads.append(
                pltpu.make_async_copy(
                    src.at[pl.ds(r, h), pl.ds(c, w)],
                    dst.at[pl.ds(r, h), pl.ds(c, w)],
                    load_sem.at[k * 5 + a],
                )
            )
    loads.append(pltpu.make_async_copy(a_in, active, load_sem.at[5 * len(regions)]))
    for copy in loads:
        copy.start()

    def messages(items, first):
        made = []
        for k, (src, dst, offset) in enumerate(items):
            made.append((
                pltpu.make_async_remote_copy(
                    src_ref=src, dst_ref=dst,
                    send_sem=send_sem.at[first + k], recv_sem=recv_sem.at[first + k],
                    device_id={"lat": lat + offset[0], "lon": lon + offset[1]},
                    device_id_type=pl.DeviceIdType.MESH,
                ),
                offset,
            ))
        return made

    def start(made):
        for copy, offset in made:
            @pl.when(has(offset))
            def _(copy=copy):
                copy.start()

    def finish(made):
        for copy, offset in made:
            @pl.when(has(opposite(offset)))
            def _(copy=copy):
                copy.wait_recv()

            @pl.when(has(offset))
            def _(copy=copy):
                copy.wait_send()

    every = pl.ds(0, 4)
    body = pl.ds(0, cols)
    first, final = pl.ds(0, WIDE), pl.ds(rows - WIDE, WIDE)
    halos = messages([
        (TOP.at[every, pl.ds(edge, edge), body], BOT.at[every, pl.ds(edge, edge), body], SOUTH),
        (BOT.at[every, pl.ds(0, edge), body], TOP.at[every, pl.ds(0, edge), body], NORTH),
        (pack_w, got_e, WEST),
        (pack_e, got_w, EAST),
        (pack_w.at[first], corner.at[3], SW),
        (pack_e.at[first], corner.at[2], SE),
        (pack_w.at[final], corner.at[1], NW),
        (pack_e.at[final], corner.at[0], NE),
        (pack_w.at[first], side.at[2], SOUTH),
        (pack_e.at[first], side.at[3], SOUTH),
        (pack_w.at[final], side.at[0], NORTH),
        (pack_e.at[final], side.at[1], NORTH),
    ], 0)

    @pl.when(lat == 0)
    def _():
        TOP[:, 0:edge, 0:cols] = jnp.zeros((4, edge, cols), F32)
        side[0:2] = jnp.zeros_like(side[0:2])
        fold[0] = jnp.zeros_like(fold[0])

    @pl.when(lat == nlat - 1)
    def _():
        BOT[:, edge : 2 * edge, 0:cols] = jnp.zeros((4, edge, cols), F32)
        side[2:4] = jnp.zeros_like(side[2:4])
        fold[1] = jnp.zeros_like(fold[1])

    for pack, offset in ((got_w, WEST), (got_e, EAST)):
        @pl.when(jnp.logical_not(has(offset)))
        def _(pack=pack):
            pack[...] = jnp.zeros_like(pack)

    for k, offset in enumerate((SW, SE, NW, NE)):
        @pl.when(jnp.logical_not(has(offset)))
        def _(k=k):
            corner[k] = jnp.zeros_like(corner[k])

    R[...] = jnp.zeros_like(R)

    def span(t):
        return slice(t * LANES, (t + 1) * LANES)

    def cell(f, r, h, t):
        return f[r : r + h, span(t)]

    def depth_of(r, h, t):
        return cell(D, r, h, t) * (0.5 * cell(W, r, h, t).astype(F32))

    for copy in loads[:10]:
        copy.wait()

    lane = lanes_of((rows, LANES))
    far = tiles - 1
    sides = {}
    for t in (0, far):
        sides[t] = [cell(f, 0, rows, t) for f in (S, E, N)] + [depth_of(0, rows, t)]

    def pick(x, pieces):
        total = pieces[-1]
        for k in (2, 1, 0):
            total = jnp.where(x < WIDE * (k + 1), pieces[k], total)
        return total

    pack_w[...] = pick(lane, [turn(sides[0][a], WIDE * a) for a in range(4)])
    pack_e[...] = pick(lane, [turn(sides[far][a], WIDE * (a - 2)) for a in (3, 0, 1, 2)])
    pl.semaphore_wait(barrier, count)
    start(halos[2:])

    for copy in loads[10:20]:
        copy.wait()
    for a, f in enumerate((S, E, N, None)):
        for t in range(tiles):
            for buffer, to, r in ((TOP, edge, 0), (BOT, 0, rows - edge)):
                v = depth_of(r, edge, t) if f is None else cell(f, r, edge, t)
                buffer[a, to : to + edge, span(t)] = v

    start(halos[:2])

    for a in range(4):
        Z[a] = jnp.where(lane < WIDE, sides[0][a], turn(sides[far][a], 2 * WIDE))

    def read(f, r=0, h=rows):
        return [cell(f, r, h, t) for t in range(tiles)]

    def write(f, x, r=0):
        for t, v in enumerate(x):
            f[r : r + v.shape[0], span(t)] = v

    n_before = None
    begin = 0
    for k, (r, h) in enumerate(chunks):
        for copy in loads[20 + 5 * k : 25 + 5 * k]:
            copy.wait()
        last = k == len(chunks) - 1
        end = rows if last else r + h - HALO
        height = end - begin
        m = [0.5 * v.astype(F32) for v in read(W, begin, height)]
        depth = [v * w for v, w in zip(read(D, begin, height), m)]
        after = (None, None, None)
        if not last:
            half = [0.5 * v.astype(F32) for v in read(W, end, HALO)]
            after = (
                read(S, end, HALO),
                [v * (w + w) for v, w in zip(read(N, end, HALO), half)],
                [v * w for v, w in zip(read(D, end, HALO), half)],
            )
        s, e, n, cx, cy = first_step(
            read(S, begin, height), read(E, begin, height), read(N, begin, height), depth, m, after, n_before
        )
        for f, x in ((S, s), (E, e), (N, n), (D, cx), (CY, cy), (M, m)):
            write(f, x, begin)
        n_before = [v[height - HALO :] for v in n]
        begin = end
    loads[-1].wait()

    for step in range(STEPS - 2):
        s, e, n = next_step(*(read(f) for f in (S, E, N, D, CY, M)))
        for f, x in ((S, s), (E, e), (N, n)):
            write(f, x)

    s, e, n = next_step(*(read(f) for f in (S, E, N, D, CY, M)))
    for f, x in ((s_out, s), (e_out, from_left(e, 1)), (n_out, down(n, 1))):
        write(f, x)

    within = (lax.broadcasted_iota(jnp.int32, (HALO, LANES), 0).astype(F32) + 0.5) / SPACING
    lower = [spline_weight(within + 1.5 - k) for k in range(4)]
    upper = [spline_weight(within + 1.0 - k) for k in range(4)]

    def total_of(x):
        return jnp.sum(x, axis=0, keepdims=True)

    cells = rows // SPACING

    def row_sums(v, t):
        none = jnp.zeros((HALO, LANES), F32)
        c = [none] * 4
        for q in range(cells):
            r = q * SPACING
            low, high = v[r : r + HALO], v[r + HALO : r + SPACING]
            a = [low * w for w in lower] if q > 0 else [none] * 4
            b = [high * w for w in upper] if q < cells - 1 else [none] * 4
            R[q : q + 1, span(t)] = total_of(c[0] + a[0])
            c = [c[1] + (a[1] + b[0]), c[2] + (a[2] + b[1]), c[3] + (a[3] + b[2]), b[3]]
        for k in range(4):
            R[cells + k : cells + k + 1, span(t)] = total_of(c[k])

    def strip_sums(v):
        none = jnp.zeros((HALO, LANES), F32)
        c = [none] * 4
        for q in range(-2, cells + 2):
            r = WIDE + q * SPACING
            low, high = v[r : r + HALO], v[r + HALO : r + SPACING]
            a = [low * w for w in lower] if q > -2 else [none] * 4
            b = [high * w for w in upper] if q < cells + 1 else [none] * 4
            if q >= 2:
                R[q : q + 1, span(tiles)] = total_of(c[0] + a[0])
            c = [c[1] + (a[1] + b[0]), c[2] + (a[2] + b[1]), c[3] + (a[3] + b[2]), b[3]]

    def inner_columns(x):
        at = lanes_of(x[0].shape)
        x[0] = jnp.where(at >= 8, x[0], 0.0)
        x[far] = jnp.where(at < LANES - 8, x[far], 0.0)
        return x

    s = inner_columns(s)
    for t in range(tiles):
        row_sums(s[t], t)

    shape = (LANES, LANES)
    at = lax.broadcasted_iota(jnp.int32, shape, 0)
    point = lanes_of(shape).astype(F32) - 2.0 + 0.5
    column_weight = spline_weight((at.astype(F32) + 0.5) / SPACING - point)
    strip_column = jnp.where(at < WIDE, at, jnp.where(at < 3 * WIDE, at + (cols - 2 * WIDE), at - LANES))
    strip_weight = spline_weight((strip_column.astype(F32) + 0.5) / SPACING - point)
    strip_weight = jnp.where((at < 8) | (at >= 2 * WIDE - 8), strip_weight, 0.0)

    def dot(x, w):
        return jnp.dot(x, w, precision=lax.Precision.HIGHEST, preferred_element_type=F32)

    def along(f):
        h = f.shape[0]
        spread = dot(jnp.concatenate([f[:, span(t)] for t in range(tiles)], axis=0), column_weight)
        total = spread[0:h]
        for t in range(1, tiles):
            total = total + turn(spread[t * h : (t + 1) * h], 8 * t)
        return total

    points = R.shape[0]
    own = along(R)
    PART[...] = own
    top, bottom = pl.ds(0, HALO), pl.ds(points - HALO, HALO)
    cross = messages([
        (PART.at[bottom], fold.at[0], NORTH),
        (PART.at[top], fold.at[1], SOUTH),
    ], len(halos))
    start(cross)

    finish(halos[:2])
    edges = [march(*([buffer[a, :, span(t)] for t in range(tiles)] for a in range(4))) for buffer in (TOP, BOT)]
    for f, south, north in zip((s_out, e_out, n_out), *edges):
        for t in range(tiles):
            f[0:HALO, span(t)] = south[t][edge : edge + HALO]
            f[rows - HALO : rows, span(t)] = north[t][HALO:edge]
    south = inner_columns([v[HALO : edge + HALO] for v in edges[0][0]])
    north = inner_columns([v[HALO : edge + HALO] for v in edges[1][0]])
    for t in range(tiles):
        for k in range(4):
            RE[k : k + 1, span(t)] = total_of(south[t][:HALO] * upper[k] + south[t][HALO:] * lower[k])
            RE[4 + k : 5 + k, span(t)] = total_of(north[t][:HALO] * upper[k] + north[t][HALO:] * lower[k])
    more = along(RE)
    none = jnp.zeros((4, LANES), F32)
    own = jnp.concatenate([
        own[:HALO] + jnp.concatenate([more[0:4], none], axis=0),
        own[HALO : points - HALO],
        own[points - HALO :] + jnp.concatenate([more[4:8], none], axis=0),
    ], axis=0)

    finish(halos[2:])
    fields = []
    for a in range(4):
        parts = []
        for last, east, west, near in (
            (side[1], corner[1], corner[0], side[0]),
            (None, got_e[...], got_w[...], None),
            (side[3], corner[3], corner[2], side[2]),
        ):
            x = lanes_of(east.shape)
            group = (x >= WIDE * a) & (x < WIDE * (a + 1))
            mine = Z[a] if last is None else turn(jnp.where(group, near, last), -WIDE * a)
            theirs = turn(jnp.where(group, east, west), WIDE * (2 - a))
            parts.append(jnp.where(x < 2 * WIDE, mine, theirs))
        fields.append([jnp.concatenate(parts, axis=0)])
    strip = [x[0] for x in march(*fields)]
    strip_sums(strip[0])
    strip = [x[WIDE : WIDE + rows] for x in strip]
    own = own + dot(R[:, span(tiles)], strip_weight)

    for f, z in zip((s_out, e_out, n_out), strip):
        f[:, span(0)] = jnp.where(lane < 8, z, f[:, span(0)])
        f[:, span(far)] = jnp.where(lane >= LANES - 8, turn(z, 2 * WIDE), f[:, span(far)])
    finish(cross)

    row = lax.broadcasted_iota(jnp.int32, (HALO, LANES), 0)
    mine = jnp.concatenate([
        own[:HALO] + jnp.where((row == 2) | (row == 3), fold[0], 0.0),
        own[HALO : points - HALO],
        own[points - HALO :] + jnp.where(row < 2, fold[1], 0.0),
    ], axis=0)
    inside = mine[2 : 2 + rows // SPACING, 2 : 2 + cols // SPACING]
    grad[...] = inside * active[...].astype(F32) / SPACING


def deliver(*refs):
    sem = refs[8]
    copies = []
    for k in range(3):
        rows = refs[k].shape[0] // PIECES
        for p in range(PIECES):
            here = pl.ds(p * rows, rows)
            copies.append(
                pltpu.make_async_copy(refs[k].at[here], refs[4 + k].at[here], sem.at[len(copies)])
            )
    copies.append(pltpu.make_async_copy(refs[3], refs[7], sem.at[len(copies)]))
    for copy in copies:
        copy.start()
    for copy in copies:
        copy.wait()


def local(surface_adjoint, east_adjoint, north_adjoint, water_depth, wet_mask, control_active):
    rows, cols = surface_adjoint.shape
    points = rows // SPACING + 4
    points = (points + 7) // 8 * 8
    field = pltpu.VMEM((rows, cols), F32)
    rim = pltpu.VMEM((4, 4 * HALO, cols), F32)
    pack = pltpu.VMEM((rows, LANES), F32)
    whole = pl.BlockSpec(memory_space=pltpu.VMEM)
    in_hbm = pl.BlockSpec(memory_space=pltpu.HBM)
    shape = jax.ShapeDtypeStruct((rows, cols), F32)
    hold = lambda x: pltpu.with_memory_space_constraint(x, pltpu.HBM)
    s, e, n, g = pl.pallas_call(
        kernel,
        out_shape=(shape, shape, shape, jax.ShapeDtypeStruct(control_active.shape, F32)),
        in_specs=[in_hbm] * 6,
        out_specs=(whole,) * 4,
        scratch_shapes=[
            field, field, field, field,
            pltpu.VMEM((rows, cols), jnp.int32),
            field, field,
            pltpu.VMEM((points, cols + LANES), F32),
            pltpu.VMEM((points, LANES), F32),
            pltpu.VMEM(control_active.shape, jnp.int32),
            rim, rim,
            pltpu.VMEM((4, rows, LANES), F32),
            pack, pack, pack, pack,
            pltpu.VMEM((4, WIDE, LANES), F32),
            pltpu.VMEM((4, WIDE, LANES), F32),
            pltpu.VMEM((2, HALO, LANES), F32),
            pltpu.VMEM((HALO, cols), F32),
            pltpu.SemaphoreType.DMA((5 * (4 + CHUNKS) + 1,)),
            pltpu.SemaphoreType.DMA((14,)),
            pltpu.SemaphoreType.DMA((14,)),
        ],
        compiler_params=pltpu.CompilerParams(
            collective_id=0, has_side_effects=True, vmem_limit_bytes=32 * 1024 * 1024
        ),
    )(hold(surface_adjoint), hold(east_adjoint), hold(north_adjoint), hold(water_depth), hold(wet_mask), hold(control_active))
    return pl.pallas_call(
        deliver,
        out_shape=(shape, shape, shape, jax.ShapeDtypeStruct(control_active.shape, F32)),
        in_specs=[whole] * 4,
        out_specs=(in_hbm,) * 4,
        scratch_shapes=[pltpu.SemaphoreType.DMA((3 * PIECES + 1,))],
    )(*[pltpu.with_memory_space_constraint(x, pltpu.VMEM) for x in (s, e, n, g)])


def solution(mesh):
    spec = P("lat", "lon")
    return jax.shard_map(
        local, mesh=mesh, in_specs=(spec,) * 6, out_specs=(spec,) * 4, check_vma=False
    )
```

```python
import jax
import jax.numpy as jnp
from jax import lax
from jax.experimental import pallas as pl
from jax.experimental.pallas import tpu as pltpu
from jax.sharding import PartitionSpec as P

SPACING = 16
LANES = 128
HALO = 8
WIDE = 32
CHUNKS = 4
PIECES = 1
STEPS = 3
F32 = jnp.float32

SOUTH, NORTH, WEST, EAST = (-1, 0), (1, 0), (0, -1), (0, 1)
SW, SE, NW, NE = (-1, -1), (-1, 1), (1, -1), (1, 1)
NEIGHBOURS = (SOUTH, NORTH, WEST, EAST, SW, SE, NW, NE)


def spline_weight(arg):
    mag = jnp.abs(arg)
    inner = 2.0 / 3.0 - mag * mag + 0.5 * mag * mag * mag
    outer = (2.0 - mag) * (2.0 - mag) * (2.0 - mag) / 6.0
    return jnp.where(mag < 1.0, inner, jnp.where(mag < 2.0, outer, 0.0 * mag))


def lanes_of(shape):
    return lax.broadcasted_iota(jnp.int32, shape, 1)


def below(x, following, k):
    return jnp.concatenate([x, following], axis=0)[k : k + x.shape[0]]


def above(preceding, x, k):
    return jnp.concatenate([preceding, x], axis=0)[HALO - k : HALO - k + x.shape[0]]


def turn(x, k):
    return pltpu.roll(x, k % LANES, axis=1) if k % LANES else x


def from_right(x, k):
    turned = [turn(v, -k) for v in x]
    if len(x) == 1:
        return turned
    at = lanes_of(x[0].shape)
    return [jnp.where(at < LANES - k, turned[t], turned[(t + 1) % len(x)]) for t in range(len(x))]


def from_left(x, k):
    turned = [turn(v, k) for v in x]
    if len(x) == 1:
        return turned
    at = lanes_of(x[0].shape)
    return [jnp.where(at >= k, turned[t], turned[t - 1]) for t in range(len(x))]


def up(x, k, following=None):
    none = jnp.zeros((HALO, LANES), F32)
    return [below(v, following[i] if following else none, k) for i, v in enumerate(x)]


def down(x, k, preceding=None):
    none = jnp.zeros((HALO, LANES), F32)
    return [above(preceding[i] if preceding else none, v, k) for i, v in enumerate(x)]


def change(s, e, n, cx, cy, s_after=None, n_before=None):
    s_right, s_up = from_right(s, 2), up(s, 2, s_after)
    e = [v + c * (r - o) for v, c, r, o in zip(e, cx, s_right, s)]
    n = [v + c * (r - o) for v, c, r, o in zip(n, cy, s_up, s)]
    flow = [(v - l) + (w - d) for v, l, w, d in zip(e, from_left(e, 2), n, down(n, 2, n_before))]
    return flow, e, n


def first_step(s, e, n, depth, m, after=(None, None, None), n_before=None):
    s_after, n_after, depth_after = after
    wet = [v + v for v in m]
    e = from_right([v * w for v, w in zip(e, wet)], 1)
    n = up([v * w for v, w in zip(n, wet)], 1, n_after)
    cx, cy = from_right(depth, 1), up(depth, 1, depth_after)
    flow, e, n = change(s, e, n, cx, cy, s_after, n_before)
    s = [w * (v + v + f) for w, v, f in zip(m, s, flow)]
    return s, e, n, cx, cy


def next_step(s, e, n, cx, cy, m):
    flow, e, n = change(s, e, n, cx, cy)
    return [v + w * f for v, w, f in zip(s, m, flow)], e, n


def march(s, e, n, depth):
    m = [jnp.where(v > 0.0, 0.5, 0.0) for v in depth]
    s, e, n, cx, cy = first_step(s, e, n, depth, m)
    for step in range(STEPS - 1):
        s, e, n = next_step(s, e, n, cx, cy, m)
    return s, from_left(e, 1), down(n, 1)


def kernel(
    s_in, e_in, n_in, d_in, w_in, a_in,
    s_out, e_out, n_out, grad,
    S, E, N, D, W, CY, M, R, PART, active,
    TOP, BOT, Z, pack_w, pack_e, got_w, got_e, corner, side, fold, RE,
    load_sem, send_sem, recv_sem,
):
    rows, cols = s_out.shape
    tiles = cols // LANES
    edge = 2 * HALO
    nlat, nlon = lax.axis_size("lat"), lax.axis_size("lon")
    lat, lon = lax.axis_index("lat"), lax.axis_index("lon")

    def has(offset):
        a, b = lat + offset[0], lon + offset[1]
        return (a >= 0) & (a < nlat) & (b >= 0) & (b < nlon)

    def opposite(offset):
        return (-offset[0], -offset[1])

    barrier = pltpu.get_barrier_semaphore()
    count = jnp.int32(0)
    for offset in NEIGHBOURS:
        count = count + has(offset).astype(jnp.int32)

        @pl.when(has(offset))
        def _(offset=offset):
            pl.semaphore_signal(
                barrier, inc=1,
                device_id={"lat": lat + offset[0], "lon": lon + offset[1]},
                device_id_type=pl.DeviceIdType.MESH,
            )

    part = (rows - 2 * edge) // (HALO * CHUNKS) * HALO
    chunks = [(edge + k * part, part) for k in range(CHUNKS - 1)]
    chunks.append((edge + (CHUNKS - 1) * part, rows - 2 * edge - (CHUNKS - 1) * part))
    regions = (
        (0, rows, 0, LANES),
        (0, rows, cols - LANES, LANES),
        (0, edge, LANES, cols - 2 * LANES),
        (rows - edge, edge, LANES, cols - 2 * LANES),
    ) + tuple((r, h, LANES, cols - 2 * LANES) for r, h in chunks)
    loads = []
    for k, (r, h, c, w) in enumerate(regions):
        for a, (src, dst) in enumerate(((w_in, W), (d_in, D), (e_in, E), (n_in, N), (s_in, S))):
            loads.append(
                pltpu.make_async_copy(
                    src.at[pl.ds(r, h), pl.ds(c, w)],
                    dst.at[pl.ds(r, h), pl.ds(c, w)],
                    load_sem.at[k * 5 + a],
                )
            )
    loads.append(pltpu.make_async_copy(a_in, active, load_sem.at[5 * len(regions)]))
    for copy in loads:
        copy.start()

    def messages(items, first):
        made = []
        for k, (src, dst, offset) in enumerate(items):
            made.append((
                pltpu.make_async_remote_copy(
                    src_ref=src, dst_ref=dst,
                    send_sem=send_sem.at[first + k], recv_sem=recv_sem.at[first + k],
                    device_id={"lat": lat + offset[0], "lon": lon + offset[1]},
                    device_id_type=pl.DeviceIdType.MESH,
                ),
                offset,
            ))
        return made

    def start(made):
        for copy, offset in made:
            @pl.when(has(offset))
            def _(copy=copy):
                copy.start()

    def finish(made):
        for copy, offset in made:
            @pl.when(has(opposite(offset)))
            def _(copy=copy):
                copy.wait_recv()

            @pl.when(has(offset))
            def _(copy=copy):
                copy.wait_send()

    every = pl.ds(0, 4)
    body = pl.ds(0, cols)
    first, final = pl.ds(0, WIDE), pl.ds(rows - WIDE, WIDE)
    halos = messages([
        (TOP.at[every, pl.ds(edge, edge), body], BOT.at[every, pl.ds(edge, edge), body], SOUTH),
        (BOT.at[every, pl.ds(0, edge), body], TOP.at[every, pl.ds(0, edge), body], NORTH),
        (pack_w, got_e, WEST),
        (pack_e, got_w, EAST),
        (pack_w.at[first], corner.at[3], SW),
        (pack_e.at[first], corner.at[2], SE),
        (pack_w.at[final], corner.at[1], NW),
        (pack_e.at[final], corner.at[0], NE),
        (pack_w.at[first], side.at[2], SOUTH),
        (pack_e.at[first], side.at[3], SOUTH),
        (pack_w.at[final], side.at[0], NORTH),
        (pack_e.at[final], side.at[1], NORTH),
    ], 0)

    @pl.when(lat == 0)
    def _():
        TOP[:, 0:edge, 0:cols] = jnp.zeros((4, edge, cols), F32)
        side[0:2] = jnp.zeros_like(side[0:2])
        fold[0] = jnp.zeros_like(fold[0])

    @pl.when(lat == nlat - 1)
    def _():
        BOT[:, edge : 2 * edge, 0:cols] = jnp.zeros((4, edge, cols), F32)
        side[2:4] = jnp.zeros_like(side[2:4])
        fold[1] = jnp.zeros_like(fold[1])

    for pack, offset in ((got_w, WEST), (got_e, EAST)):
        @pl.when(jnp.logical_not(has(offset)))
        def _(pack=pack):
            pack[...] = jnp.zeros_like(pack)

    for k, offset in enumerate((SW, SE, NW, NE)):
        @pl.when(jnp.logical_not(has(offset)))
        def _(k=k):
            corner[k] = jnp.zeros_like(corner[k])

    R[...] = jnp.zeros_like(R)

    def span(t):
        return slice(t * LANES, (t + 1) * LANES)

    def cell(f, r, h, t):
        return f[r : r + h, span(t)]

    def depth_of(r, h, t):
        return cell(D, r, h, t) * (0.5 * cell(W, r, h, t).astype(F32))

    for copy in loads[:10]:
        copy.wait()

    lane = lanes_of((rows, LANES))
    far = tiles - 1
    sides = {}
    for t in (0, far):
        sides[t] = [cell(f, 0, rows, t) for f in (S, E, N)] + [depth_of(0, rows, t)]

    def pick(x, pieces):
        total = pieces[-1]
        for k in (2, 1, 0):
            total = jnp.where(x < WIDE * (k + 1), pieces[k], total)
        return total

    pack_w[...] = pick(lane, [turn(sides[0][a], WIDE * a) for a in range(4)])
    pack_e[...] = pick(lane, [turn(sides[far][a], WIDE * (a - 2)) for a in (3, 0, 1, 2)])
    for copy in loads[10:20]:
        copy.wait()
    for a, f in enumerate((S, E, N, None)):
        for t in range(tiles):
            for buffer, to, r in ((TOP, edge, 0), (BOT, 0, rows - edge)):
                v = depth_of(r, edge, t) if f is None else cell(f, r, edge, t)
                buffer[a, to : to + edge, span(t)] = v

    for a in range(4):
        Z[a] = jnp.where(lane < WIDE, sides[0][a], turn(sides[far][a], 2 * WIDE))

    def read(f, r=0, h=rows):
        return [cell(f, r, h, t) for t in range(tiles)]

    def write(f, x, r=0):
        for t, v in enumerate(x):
            f[r : r + v.shape[0], span(t)] = v

    pl.semaphore_wait(barrier, count)
    start(halos[2:])
    start(halos[:2])

    n_before = None
    begin = 0
    for k, (r, h) in enumerate(chunks):
        for copy in loads[20 + 5 * k : 25 + 5 * k]:
            copy.wait()
        last = k == len(chunks) - 1
        end = rows if last else r + h - HALO
        height = end - begin
        m = [0.5 * v.astype(F32) for v in read(W, begin, height)]
        depth = [v * w for v, w in zip(read(D, begin, height), m)]
        after = (None, None, None)
        if not last:
            half = [0.5 * v.astype(F32) for v in read(W, end, HALO)]
            after = (
                read(S, end, HALO),
                [v * (w + w) for v, w in zip(read(N, end, HALO), half)],
                [v * w for v, w in zip(read(D, end, HALO), half)],
            )
        s, e, n, cx, cy = first_step(
            read(S, begin, height), read(E, begin, height), read(N, begin, height), depth, m, after, n_before
        )
        for f, x in ((S, s), (E, e), (N, n), (D, cx), (CY, cy), (M, m)):
            write(f, x, begin)
        n_before = [v[height - HALO :] for v in n]
        begin = end
    loads[-1].wait()

    for step in range(STEPS - 2):
        s, e, n = next_step(*(read(f) for f in (S, E, N, D, CY, M)))
        for f, x in ((S, s), (E, e), (N, n)):
            write(f, x)

    s, e, n = next_step(*(read(f) for f in (S, E, N, D, CY, M)))
    for f, x in ((s_out, s), (e_out, from_left(e, 1)), (n_out, down(n, 1))):
        write(f, x)

    within = (lax.broadcasted_iota(jnp.int32, (HALO, LANES), 0).astype(F32) + 0.5) / SPACING
    lower = [spline_weight(within + 1.5 - k) for k in range(4)]
    upper = [spline_weight(within + 1.0 - k) for k in range(4)]

    def total_of(x):
        return jnp.sum(x, axis=0, keepdims=True)

    cells = rows // SPACING

    def row_sums(v, t):
        none = jnp.zeros((HALO, LANES), F32)
        c = [none] * 4
        for q in range(cells):
            r = q * SPACING
            low, high = v[r : r + HALO], v[r + HALO : r + SPACING]
            a = [low * w for w in lower] if q > 0 else [none] * 4
            b = [high * w for w in upper] if q < cells - 1 else [none] * 4
            R[q : q + 1, span(t)] = total_of(c[0] + a[0])
            c = [c[1] + (a[1] + b[0]), c[2] + (a[2] + b[1]), c[3] + (a[3] + b[2]), b[3]]
        for k in range(4):
            R[cells + k : cells + k + 1, span(t)] = total_of(c[k])

    def strip_sums(v):
        none = jnp.zeros((HALO, LANES), F32)
        c = [none] * 4
        for q in range(-2, cells + 2):
            r = WIDE + q * SPACING
            low, high = v[r : r + HALO], v[r + HALO : r + SPACING]
            a = [low * w for w in lower] if q > -2 else [none] * 4
            b = [high * w for w in upper] if q < cells + 1 else [none] * 4
            if q >= 2:
                R[q : q + 1, span(tiles)] = total_of(c[0] + a[0])
            c = [c[1] + (a[1] + b[0]), c[2] + (a[2] + b[1]), c[3] + (a[3] + b[2]), b[3]]

    def inner_columns(x):
        at = lanes_of(x[0].shape)
        x[0] = jnp.where(at >= 8, x[0], 0.0)
        x[far] = jnp.where(at < LANES - 8, x[far], 0.0)
        return x

    s = inner_columns(s)
    for t in range(tiles):
        row_sums(s[t], t)

    shape = (LANES, LANES)
    at = lax.broadcasted_iota(jnp.int32, shape, 0)
    point = lanes_of(shape).astype(F32) - 2.0 + 0.5
    column_weight = spline_weight((at.astype(F32) + 0.5) / SPACING - point)
    strip_column = jnp.where(at < WIDE, at, jnp.where(at < 3 * WIDE, at + (cols - 2 * WIDE), at - LANES))
    strip_weight = spline_weight((strip_column.astype(F32) + 0.5) / SPACING - point)
    strip_weight = jnp.where((at < 8) | (at >= 2 * WIDE - 8), strip_weight, 0.0)

    def dot(x, w):
        return jnp.dot(x, w, precision=lax.Precision.HIGHEST, preferred_element_type=F32)

    def along(f):
        h = f.shape[0]
        spread = dot(jnp.concatenate([f[:, span(t)] for t in range(tiles)], axis=0), column_weight)
        total = spread[0:h]
        for t in range(1, tiles):
            total = total + turn(spread[t * h : (t + 1) * h], 8 * t)
        return total

    points = R.shape[0]
    own = along(R)
    PART[...] = own
    top, bottom = pl.ds(0, HALO), pl.ds(points - HALO, HALO)
    cross = messages([
        (PART.at[bottom], fold.at[0], NORTH),
        (PART.at[top], fold.at[1], SOUTH),
    ], len(halos))
    start(cross)

    finish(halos[:2])
    edges = [march(*([buffer[a, :, span(t)] for t in range(tiles)] for a in range(4))) for buffer in (TOP, BOT)]
    for f, south, north in zip((s_out, e_out, n_out), *edges):
        for t in range(tiles):
            f[0:HALO, span(t)] = south[t][edge : edge + HALO]
            f[rows - HALO : rows, span(t)] = north[t][HALO:edge]
    south = inner_columns([v[HALO : edge + HALO] for v in edges[0][0]])
    north = inner_columns([v[HALO : edge + HALO] for v in edges[1][0]])
    for t in range(tiles):
        for k in range(4):
            RE[k : k + 1, span(t)] = total_of(south[t][:HALO] * upper[k] + south[t][HALO:] * lower[k])
            RE[4 + k : 5 + k, span(t)] = total_of(north[t][:HALO] * upper[k] + north[t][HALO:] * lower[k])
    more = along(RE)
    none = jnp.zeros((4, LANES), F32)
    own = jnp.concatenate([
        own[:HALO] + jnp.concatenate([more[0:4], none], axis=0),
        own[HALO : points - HALO],
        own[points - HALO :] + jnp.concatenate([more[4:8], none], axis=0),
    ], axis=0)

    finish(halos[2:])
    fields = []
    for a in range(4):
        parts = []
        for last, east, west, near in (
            (side[1], corner[1], corner[0], side[0]),
            (None, got_e[...], got_w[...], None),
            (side[3], corner[3], corner[2], side[2]),
        ):
            x = lanes_of(east.shape)
            group = (x >= WIDE * a) & (x < WIDE * (a + 1))
            mine = Z[a] if last is None else turn(jnp.where(group, near, last), -WIDE * a)
            theirs = turn(jnp.where(group, east, west), WIDE * (2 - a))
            parts.append(jnp.where(x < 2 * WIDE, mine, theirs))
        fields.append([jnp.concatenate(parts, axis=0)])
    strip = [x[0] for x in march(*fields)]
    strip_sums(strip[0])
    strip = [x[WIDE : WIDE + rows] for x in strip]
    own = own + dot(R[:, span(tiles)], strip_weight)

    for f, z in zip((s_out, e_out, n_out), strip):
        f[:, span(0)] = jnp.where(lane < 8, z, f[:, span(0)])
        f[:, span(far)] = jnp.where(lane >= LANES - 8, turn(z, 2 * WIDE), f[:, span(far)])
    finish(cross)

    row = lax.broadcasted_iota(jnp.int32, (HALO, LANES), 0)
    mine = jnp.concatenate([
        own[:HALO] + jnp.where((row == 2) | (row == 3), fold[0], 0.0),
        own[HALO : points - HALO],
        own[points - HALO :] + jnp.where(row < 2, fold[1], 0.0),
    ], axis=0)
    inside = mine[2 : 2 + rows // SPACING, 2 : 2 + cols // SPACING]
    grad[...] = inside * active[...].astype(F32) / SPACING


def deliver(*refs):
    sem = refs[8]
    copies = []
    for k in range(3):
        rows = refs[k].shape[0] // PIECES
        for p in range(PIECES):
            here = pl.ds(p * rows, rows)
            copies.append(
                pltpu.make_async_copy(refs[k].at[here], refs[4 + k].at[here], sem.at[len(copies)])
            )
    copies.append(pltpu.make_async_copy(refs[3], refs[7], sem.at[len(copies)]))
    for copy in copies:
        copy.start()
    for copy in copies:
        copy.wait()


def local(surface_adjoint, east_adjoint, north_adjoint, water_depth, wet_mask, control_active):
    rows, cols = surface_adjoint.shape
    points = rows // SPACING + 4
    points = (points + 7) // 8 * 8
    field = pltpu.VMEM((rows, cols), F32)
    rim = pltpu.VMEM((4, 4 * HALO, cols), F32)
    pack = pltpu.VMEM((rows, LANES), F32)
    whole = pl.BlockSpec(memory_space=pltpu.VMEM)
    in_hbm = pl.BlockSpec(memory_space=pltpu.HBM)
    shape = jax.ShapeDtypeStruct((rows, cols), F32)
    hold = lambda x: pltpu.with_memory_space_constraint(x, pltpu.HBM)
    s, e, n, g = pl.pallas_call(
        kernel,
        out_shape=(shape, shape, shape, jax.ShapeDtypeStruct(control_active.shape, F32)),
        in_specs=[in_hbm] * 6,
        out_specs=(whole,) * 4,
        scratch_shapes=[
            field, field, field, field,
            pltpu.VMEM((rows, cols), jnp.int32),
            field, field,
            pltpu.VMEM((points, cols + LANES), F32),
            pltpu.VMEM((points, LANES), F32),
            pltpu.VMEM(control_active.shape, jnp.int32),
            rim, rim,
            pltpu.VMEM((4, rows, LANES), F32),
            pack, pack, pack, pack,
            pltpu.VMEM((4, WIDE, LANES), F32),
            pltpu.VMEM((4, WIDE, LANES), F32),
            pltpu.VMEM((2, HALO, LANES), F32),
            pltpu.VMEM((HALO, cols), F32),
            pltpu.SemaphoreType.DMA((5 * (4 + CHUNKS) + 1,)),
            pltpu.SemaphoreType.DMA((14,)),
            pltpu.SemaphoreType.DMA((14,)),
        ],
        compiler_params=pltpu.CompilerParams(
            collective_id=0, has_side_effects=True, vmem_limit_bytes=32 * 1024 * 1024
        ),
    )(hold(surface_adjoint), hold(east_adjoint), hold(north_adjoint), hold(water_depth), hold(wet_mask), hold(control_active))
    return pl.pallas_call(
        deliver,
        out_shape=(shape, shape, shape, jax.ShapeDtypeStruct(control_active.shape, F32)),
        in_specs=[whole] * 4,
        out_specs=(in_hbm,) * 4,
        scratch_shapes=[pltpu.SemaphoreType.DMA((3 * PIECES + 1,))],
    )(*[pltpu.with_memory_space_constraint(x, pltpu.VMEM) for x in (s, e, n, g)])


def solution(mesh):
    spec = P("lat", "lon")
    return jax.shard_map(
        local, mesh=mesh, in_specs=(spec,) * 6, out_specs=(spec,) * 4, check_vma=False
    )
```
